32 devices in a mesh: grp: 2 (over y), tok: 16 (over z, x, core).
Axes of the slice: x: 2, y: 2, z: 4, core: 2. Of those that a mesh axis runs over, the one named last changes fastest.
Arguments:
- hidden: bfloat16 [4, 1024, 1536], P('grp', 'tok'), parts along dimension 0
- base_ids: int32 [4, 1024], P('grp', 'tok'), parts along dimension 0, may hold values from 0 to 4, as said below
- attn_gain: bfloat16 [1536], replicated, may hold values from 0.099609375 to 1.8984375
- q_weight: bfloat16 [1536, 768], replicated
- kv_weight: bfloat16 [1536, 384], replicated
- out_weight: bfloat16 [768, 1536], replicated, may hold values from -0.21875 to 0.21875
- head_gain: bfloat16 [1536], replicated, may hold values from 0.099609375 to 1.8984375
- head_weight: bfloat16 [1536, 1536], replicated, may hold values from -0.15625 to 0.15625
- head_bias: float32 [1536], replicated, may hold values from -1 to 1
- track_perm: int32 [1536], replicated, may hold values from 0 to 1535, each once
Outputs:
- combined: float32 [2048, 1536], P(('grp', 'tok')), parts along dimension 0
The draws below stay inside these ranges and needn't reach their ends.
There are 2 independent parts, one for each index of `grp`. The reference program is written for one: setup_inputs(seed, part) draws one part's arguments, and reference() takes and returns one part's arrays. A program takes and returns all parts, laid end to end along the dimension named above; an argument that names none is the same for every part. Nothing has to cross between parts.
Inputs may be any that keep to these rules, and one draw needn't show every extreme that they name: `base_ids`: every eighth token of each strand, from token 0, has a base 0 to 3.
All inputs are finite; a program needn't handle non-finite values.
Results may differ from the reference program's by a relative error of at most 0.0058.
Values may be sent and summed in bfloat16 or wider, within the bound.
No kernel may reach another device: no remote copies, remote signals or barrier semaphores. Data moves between devices by JAX's collectives and lax.ppermute only.
A program may use at most 128 MiB of HBM per device.

```python
import math
import jax
import jax.numpy as jnp
from jax import lax

D = 1536
HEADS = 4
DH = 192
TRACKS = 1536
TOK_DEV = 64
LENGTH = 1024
N_TOK = 16


def shared_key_cols(key):
    return jax.random.normal(jax.random.fold_in(key, 11), (D, DH), jnp.float32) * D ** (-0.5)


def draw_kv_weight(key, part):
    key_cols = shared_key_cols(key)
    value_cols = jax.random.normal(jax.random.fold_in(key, 12), (D, DH), jnp.float32) * D ** (-0.5)
    return jnp.concatenate([key_cols, value_cols], axis=1).astype(jnp.bfloat16)


def draw_q_weight(key, part):
    jitter = jax.random.normal(jax.random.fold_in(key, 13), (D, HEADS, DH), jnp.float32) * D ** (-0.5)
    result = jitter
    return result.reshape(D, HEADS * DH).astype(jnp.bfloat16)


def draw_hidden(key, part):
    result = jax.random.normal(jax.random.fold_in(key, 24), (2, LENGTH, D), jnp.float32)
    return result.astype(jnp.bfloat16)


def draw_base_ids(key, part):
    raw_ids = jax.random.randint(jax.random.fold_in(key, 31), (2, LENGTH), 0, 5)
    safe_ids = jax.random.randint(jax.random.fold_in(key, 32), (2, LENGTH), 0, 4)
    position = jnp.arange(LENGTH)[None, :]
    return jnp.where(position % 8 == 0, safe_ids, raw_ids).astype(jnp.int32)


def noise(own_key, dims, deviation, bound, kind=jnp.bfloat16):
    values = deviation * jax.random.normal(own_key, dims, jnp.float32)
    return jnp.clip(values, min=-bound, max=bound).astype(kind)


def setup_inputs(seed: int = 0, part: int = 0) -> dict:
    key_of = jax.random.split(jax.random.key(seed), 11)
    part_keys = jax.random.split(jax.random.fold_in(key_of[10], part), 11)
    return {
        "hidden": draw_hidden(jax.random.fold_in(jax.random.fold_in(key_of[10], part), 71), part),
        "base_ids": draw_base_ids(jax.random.fold_in(jax.random.fold_in(key_of[10], part), 71), part),
        "attn_gain": jnp.clip(1.0 + 0.18 * jax.random.normal(key_of[2], (D,), jnp.float32), 0.099609375, 1.8984375).astype(jnp.bfloat16),
        "q_weight": draw_q_weight(jax.random.fold_in(key_of[10], 71), part),
        "kv_weight": draw_kv_weight(jax.random.fold_in(key_of[10], 71), part),
        "out_weight": noise(key_of[5], (HEADS * DH, D), (HEADS * DH) ** -0.5, 0.21875),
        "head_gain": jnp.clip(1.0 + 0.18 * jax.random.normal(key_of[6], (D,), jnp.float32), 0.099609375, 1.8984375).astype(jnp.bfloat16),
        "head_weight": noise(key_of[7], (D, TRACKS), D ** -0.5, 0.15625),
        "head_bias": jnp.clip(jax.random.uniform(key_of[8], (TRACKS,), jnp.float32, -1.0, 1.0), -1.0, 1.0),
        "track_perm": jax.random.permutation(key_of[9], TRACKS).astype(jnp.int32),
    }


def normalize(rows, gain):
    widened = rows.astype(jnp.float32)
    return widened * lax.rsqrt(lax.optimization_barrier(jnp.mean(widened * widened, -1, keepdims=True)) + 1e-06) * gain.astype(jnp.float32)

def reference(hidden, base_ids, attn_gain, q_weight, kv_weight, out_weight, head_gain, head_weight, head_bias, track_perm):
    score_scale = 1.0 / math.sqrt(DH)
    predictions = []
    for strand in range(2):
        normed = normalize(hidden[strand], attn_gain).astype(jnp.bfloat16)
        queries = jnp.dot(normed, q_weight, preferred_element_type=jnp.float32).astype(jnp.bfloat16)
        queries = queries.reshape(N_TOK, TOK_DEV * HEADS, DH)
        key_value = jnp.dot(normed, kv_weight, preferred_element_type=jnp.float32).astype(jnp.bfloat16)
        key_rows = key_value[:, :DH]
        value_rows = key_value[:, DH:]
        usable = (base_ids[strand] != 4)[None, :]

        def query_block(query_rows):
            scores = jnp.dot(query_rows, key_rows.T, preferred_element_type=jnp.float32) * score_scale
            scores = jnp.where(usable, scores, jnp.float32(-1e+30))
            maxima = lax.optimization_barrier(jnp.max(scores, -1, keepdims=True))
            weight_exp = jnp.where(usable, jnp.exp(scores - maxima), jnp.float32(0.0))
            totals = lax.optimization_barrier(jnp.sum(weight_exp, -1, keepdims=True))
            rounded = lax.optimization_barrier(weight_exp.astype(jnp.bfloat16))
            summed = jnp.dot(rounded, value_rows, preferred_element_type=jnp.float32)
            return (summed / totals).astype(jnp.bfloat16)
        attended = lax.map(query_block, queries).reshape(LENGTH, HEADS * DH)
        residual_sum = hidden[strand].astype(jnp.float32) + jnp.dot(attended, out_weight, preferred_element_type=jnp.float32)
        normed_out = normalize(residual_sum, head_gain).astype(jnp.bfloat16)
        track_logits = jnp.dot(normed_out, head_weight, preferred_element_type=jnp.float32) + head_bias
        predictions.append(jax.nn.softplus(track_logits).astype(jnp.bfloat16))
    reverse_side = predictions[1][::-1][:, track_perm]
    return 0.5 * (predictions[0].astype(jnp.float32) + reverse_side.astype(jnp.float32))
```

```python
import functools
import math

import jax
import jax.numpy as jnp
from jax import lax
from jax.experimental import pallas as pl
from jax.experimental.pallas import tpu as pltpu
from jax.sharding import PartitionSpec as P

VMEM = pl.BlockSpec(memory_space=pltpu.VMEM)
SMEM = pl.BlockSpec(memory_space=pltpu.SMEM)
ANY = pl.BlockSpec(memory_space=pl.ANY)
F32 = jnp.float32
BF16 = jnp.bfloat16


def exchange(value, mask):
    count = lax.axis_size("tok")
    return lax.ppermute(value, "tok", [(s, s ^ mask) for s in range(count)])


def normalize(rows, gain):
    mean = jnp.mean(rows * rows, -1, keepdims=True)
    return (rows * lax.rsqrt(mean + 1e-06) * gain).astype(BF16)


def project_kernel(core_ref, own_ref, got_ref, own_ids_ref, got_ids_ref, gain_ref, weight_ref, kv_ref, rows_ref):
    core = core_ref[0]
    tokens = own_ref.shape[1]
    head = weight_ref.shape[1] // 2
    gain = gain_ref[...].astype(F32)
    row = lax.broadcasted_iota(jnp.int32, (tokens, tokens), 0)
    col = lax.broadcasted_iota(jnp.int32, (tokens, tokens), 1)
    source = jnp.where(core == 0, row, tokens - 1 - row)
    turn = jnp.where(col == source, 1.0, 0.0).astype(BF16)
    lane = lax.broadcasted_iota(jnp.int32, (tokens, weight_ref.shape[1]), 1)
    normed = []
    hidden_flags = []
    for part, (ref, ids_ref) in enumerate(((own_ref, own_ids_ref), (got_ref, got_ids_ref))):
        block = ref[core]
        ids = jnp.where(core == 0, ids_ref[0:1, :], ids_ref[1:2, :])
        unknown = jnp.where((row == col) & (ids == 4), 1.0, 0.0)
        hidden_flags.append(jnp.max(unknown, -1, keepdims=True))
        normed.append(normalize(block.astype(F32), gain))
        rows_ref[pl.ds(part * tokens, tokens), :] = jnp.dot(
            turn, block, preferred_element_type=F32
        ).astype(BF16)
    kv = jnp.dot(jnp.concatenate(normed, 0), weight_ref[...], preferred_element_type=F32)
    for part in range(2):
        left_out = (lane < head) & (hidden_flags[part] > 0.5)
        kv_ref[pl.ds(part * tokens, tokens), :] = jnp.where(
            left_out, jnp.nan, kv[part * tokens : (part + 1) * tokens]
        ).astype(BF16)


def project(core, own, got, own_ids, got_ids, gain, weight):
    tokens, width = own.shape[1:]
    return pl.pallas_call(
        project_kernel,
        out_shape=(
            jax.ShapeDtypeStruct((2 * tokens, weight.shape[1]), BF16),
            jax.ShapeDtypeStruct((2 * tokens, width), BF16),
        ),
        in_specs=[SMEM] + [VMEM] * 6,
        out_specs=(VMEM, VMEM),
        compiler_params=pltpu.CompilerParams(vmem_limit_bytes=16 << 20),
        cost_estimate=pl.CostEstimate(
            flops=4 * tokens * width * weight.shape[1], bytes_accessed=2 * weight.size, transcendentals=0
        ),
        name="project",
    )(core, own, got, own_ids, got_ids, gain, weight)


def block_kernel(count, heads, core_ref, rows_ref, *refs):
    kv_refs = refs[:count]
    (gain_ref, head_gain_ref, bias_ref, wq_hbm, wo_hbm, wh_hbm, keep_ref, send_ref) = refs[count : count + 8]
    wq, wo, wh, kv, queries, attended, predictions, sems = refs[count + 8 :]
    copies = [
        pltpu.make_async_copy(wq_hbm, wq, sems.at[0]),
        pltpu.make_async_copy(wo_hbm, wo, sems.at[1]),
        pltpu.make_async_copy(wh_hbm, wh, sems.at[2]),
    ]
    for copy in copies:
        copy.start()
    core = core_ref[0]
    head = kv.shape[1] // 2
    tokens = rows_ref.shape[0]
    start = 0
    for ref in kv_refs:
        kv[pl.ds(start, ref.shape[0]), :] = ref[...]
        start += ref.shape[0]
    length = start
    rows = rows_ref[...].astype(F32)
    normed = normalize(rows, gain_ref[...].astype(F32))
    copies[0].wait()
    queries[...] = jnp.dot(normed, wq[...], preferred_element_type=F32).astype(BF16)
    scale = 1.0 / math.sqrt(head)
    chunk = min(length, 1024)
    for number in range(heads):
        query = queries[:, number * head : (number + 1) * head]

        def step(position, state):
            maxima, totals, summed = state
            at = pl.multiple_of(position * chunk, chunk)
            part = kv[pl.ds(at, chunk), :]
            scores = lax.dot_general(
                query, part[:, :head], (((1,), (1,)), ((), ())), preferred_element_type=F32
            )
            scores = jnp.where(scores == scores, scores * scale, -1e30)
            higher = jnp.maximum(maxima, jnp.max(scores, -1, keepdims=True))
            weights = jnp.exp(scores - higher)
            kept = jnp.exp(maxima - higher)
            totals = totals * kept + jnp.sum(weights, -1, keepdims=True)
            summed = summed * kept + jnp.dot(
                weights.astype(BF16), part[:, head:], preferred_element_type=F32
            )
            return higher, totals, summed

        state = (
            jnp.full((tokens, 1), -1e30, F32),
            jnp.zeros((tokens, 1), F32),
            jnp.zeros((tokens, head), F32),
        )
        if length == chunk:
            state = step(0, state)
        else:
            state = lax.fori_loop(0, length // chunk, step, state)
        attended[:, number * head : (number + 1) * head] = (state[2] / state[1]).astype(BF16)
    copies[1].wait()
    summed = rows + jnp.dot(attended[...], wo[...], preferred_element_type=F32)
    normed_out = normalize(summed, head_gain_ref[...].astype(F32))
    copies[2].wait()
    tracks = wh.shape[1]
    width = 256
    for at in range(0, tracks, width):
        logits = jnp.dot(normed_out, wh[:, at : at + width], preferred_element_type=F32)
        logits = logits + bias_ref[:, at : at + width]
        soft = jnp.maximum(logits, 0.0) + jnp.log1p(jnp.exp(-jnp.abs(logits)))
        predictions[:, at : at + width] = soft.astype(BF16)
    half = tokens // 2
    keep_ref[...] = predictions[pl.ds(pl.multiple_of(core * half, half), half), :]
    send_ref[...] = predictions[pl.ds(pl.multiple_of((1 - core) * half, half), half), :]


def transform(core, rows, kvs, gain, head_gain, bias, wq, wo, wh):
    tokens, width = rows.shape
    head = kvs[0].shape[1] // 2
    heads = wq.shape[1] // head
    length = sum(kv.shape[0] for kv in kvs)
    tracks = wh.shape[1]
    flops = 2 * tokens * (width * wq.shape[1] * 2 + width * tracks + 2 * length * wq.shape[1])
    return pl.pallas_call(
        functools.partial(block_kernel, len(kvs), heads),
        out_shape=(jax.ShapeDtypeStruct((tokens // 2, tracks), BF16),) * 2,
        in_specs=[SMEM] + [VMEM] * (4 + len(kvs)) + [ANY] * 3,
        out_specs=(VMEM, VMEM),
        scratch_shapes=[
            pltpu.VMEM(wq.shape, BF16),
            pltpu.VMEM(wo.shape, BF16),
            pltpu.VMEM(wh.shape, BF16),
            pltpu.VMEM((length, 2 * head), BF16),
            pltpu.VMEM((tokens, heads * head), BF16),
            pltpu.VMEM((tokens, heads * head), BF16),
            pltpu.VMEM((tokens, tracks), BF16),
            pltpu.SemaphoreType.DMA((3,)),
        ],
        compiler_params=pltpu.CompilerParams(vmem_limit_bytes=40 << 20),
        cost_estimate=pl.CostEstimate(
            flops=flops, bytes_accessed=2 * (wq.size + wo.size + wh.size), transcendentals=tokens * length * heads
        ),
        name="transform",
    )(core, rows, *kvs, gain, head_gain, bias, wq, wo, wh)


def combine_kernel(core_ref, keep_ref, got_ref, perm_ref, out_ref):
    forward_here = core_ref[0] == 0
    tracks = perm_ref.shape[1]
    tokens = keep_ref.shape[0]
    lanes = 128
    keep = keep_ref[...].astype(F32)
    got = got_ref[...].astype(F32)
    forward = jnp.where(forward_here, keep, got)
    reverse = jnp.where(forward_here, got, keep)
    for at in range(0, tracks, lanes):
        perm = jnp.broadcast_to(perm_ref[:, at : at + lanes], (tokens, lanes))
        within = perm & (lanes - 1)
        tile = perm >> 7
        picked = jnp.zeros((tokens, lanes), F32)
        for number in range(tracks // lanes):
            source = reverse[:, number * lanes : (number + 1) * lanes]
            found = jnp.take_along_axis(source, within, axis=1)
            picked = jnp.where(tile == number, found, picked)
        out_ref[:, at : at + lanes] = 0.5 * (forward[:, at : at + lanes] + picked)


def combine(core, keep, got, perm):
    return pl.pallas_call(
        combine_kernel,
        out_shape=jax.ShapeDtypeStruct(keep.shape, F32),
        in_specs=[SMEM] + [VMEM] * 3,
        out_specs=VMEM,
        compiler_params=pltpu.CompilerParams(vmem_limit_bytes=16 << 20),
        name="combine",
    )(core, keep, got, perm)


def gathered(kv):
    count = lax.axis_size("tok")
    if count > 16:
        mask = 2
        while mask < count:
            kv = jnp.concatenate([kv, exchange(kv, mask)], 0)
            mask *= 2
        return [kv]
    blocks = [kv] + [exchange(kv, mask) for mask in range(4, count, 4)]
    if count > 2:
        blocks += [exchange(block, 2) for block in blocks]
    return blocks


def per_device(
    hidden,
    base_ids,
    attn_gain,
    q_weight,
    kv_weight,
    out_weight,
    head_gain,
    head_weight,
    head_bias,
    track_perm,
):
    count = lax.axis_size("tok")
    core = (lax.axis_index("tok") % 2).astype(jnp.int32).reshape(1)
    got = exchange(hidden, 1)
    got_ids = exchange(base_ids, 1)
    gain = attn_gain.reshape(1, -1)
    kv, rows = project(core, hidden, got, base_ids, got_ids, gain, kv_weight)
    rows = lax.ppermute(
        rows, "tok", [(s, s if s % 2 == 0 else count - s) for s in range(count)]
    )
    keep, send = transform(
        core,
        rows,
        gathered(kv),
        gain,
        head_gain.reshape(1, -1),
        head_bias.reshape(1, -1),
        q_weight,
        out_weight,
        head_weight,
    )
    return combine(core, keep, exchange(send, 1), track_perm.reshape(1, -1))


def solution(mesh):
    placed = (P("grp", "tok", None), P("grp", "tok"), P(), P(), P(), P(), P(), P(), P(), P())
    return jax.shard_map(
        per_device, mesh=mesh, in_specs=placed, out_specs=P(("grp", "tok"), None), check_vma=False
    )
```

```python
import functools
import math

import jax
import jax.numpy as jnp
from jax import lax
from jax.experimental import pallas as pl
from jax.experimental.pallas import tpu as pltpu
from jax.sharding import PartitionSpec as P

VMEM = pl.BlockSpec(memory_space=pltpu.VMEM)
SMEM = pl.BlockSpec(memory_space=pltpu.SMEM)
HBM = pl.BlockSpec(memory_space=pltpu.HBM)
F32 = jnp.float32
BF16 = jnp.bfloat16


def exchange(value, mask):
    count = lax.axis_size("tok")
    return lax.ppermute(value, "tok", [(s, s ^ mask) for s in range(count)])


def normalize(rows, gain):
    mean = jnp.mean(rows * rows, -1, keepdims=True)
    return (rows * lax.rsqrt(mean + 1e-06) * gain).astype(BF16)


def project_kernel(core_ref, got_ref, got_ids_ref, *refs):
    *sources, kv_ref = refs[:5]
    own, own_ids_ref, gain_ref, weight, sems = refs[5:]
    core = core_ref[0]
    sources[0] = sources[0].at[core]
    copies = [
        pltpu.make_async_copy(source, target, sems.at[number])
        for number, (source, target) in enumerate(zip(sources, (own, own_ids_ref, gain_ref, weight)))
    ]
    for copy in copies:
        copy.start()
    tokens = own.shape[0]
    head = weight.shape[1] // 2
    row = lax.broadcasted_iota(jnp.int32, (tokens, tokens), 0)
    col = lax.broadcasted_iota(jnp.int32, (tokens, tokens), 1)
    copies[1].wait()
    copies[2].wait()
    gain = gain_ref[...].astype(F32).reshape(1, -1)
    lane = lax.broadcasted_iota(jnp.int32, (tokens, weight.shape[1]), 1)
    left_out = []
    for ids_ref in (own_ids_ref, got_ids_ref):
        ids = jnp.where(core == 0, ids_ref[0:1, :], ids_ref[1:2, :])
        unknown = jnp.where((row == col) & (ids == 4), 1.0, 0.0)
        left_out.append((lane < head) & (jnp.max(unknown, -1, keepdims=True) > 0.5))
    got_normed = normalize(got_ref[core].astype(F32), gain)
    copies[0].wait()
    normed = jnp.concatenate([normalize(own[...].astype(F32), gain), got_normed], 0)
    copies[3].wait()
    kv = jnp.dot(normed, weight[...], preferred_element_type=F32)
    for part in range(2):
        kv_ref[pl.ds(part * tokens, tokens), :] = jnp.where(
            left_out[part], jnp.nan, kv[part * tokens : (part + 1) * tokens]
        ).astype(BF16)


def project(core, own, got, own_ids, got_ids, gain, weight):
    tokens, width = own.shape[1:]
    return pl.pallas_call(
        project_kernel,
        out_shape=jax.ShapeDtypeStruct((2 * tokens, weight.shape[1]), BF16),
        in_specs=[SMEM, VMEM, VMEM] + [HBM] * 4,
        out_specs=VMEM,
        scratch_shapes=[
            pltpu.VMEM((tokens, width), BF16),
            pltpu.VMEM(own_ids.shape, jnp.int32),
            pltpu.VMEM(gain.shape, BF16),
            pltpu.VMEM(weight.shape, BF16),
            pltpu.SemaphoreType.DMA((4,)),
        ],
        compiler_params=pltpu.CompilerParams(vmem_limit_bytes=52 << 20),
        cost_estimate=pl.CostEstimate(
            flops=4 * tokens * width * weight.shape[1], bytes_accessed=2 * weight.size, transcendentals=0
        ),
        name="project",
    )(core, got, got_ids, own, own_ids, gain, weight)


def block_kernel(count, heads, core_ref, *refs):
    kv_refs = refs[:count]
    got_ref, mirrored_ref, passed_ref = refs[count : count + 3]
    own_hbm, gain_hbm, wq_hbm, wo_hbm, head_gain_hbm, wh_hbm, bias_hbm = refs[count + 3 : count + 10]
    keep_ref, send_ref = refs[count + 10 : count + 12]
    own, gain_ref, wq, wo, head_gain_ref, wh, bias_ref = refs[count + 12 : count + 19]
    kv, queries, attended, predictions, sems = refs[count + 19 :]
    groups = 2
    split = wq.shape[1] // groups
    own_copy = pltpu.make_async_copy(own_hbm.at[0], own, sems.at[0])
    wq_copies = [
        pltpu.make_async_copy(
            wq_hbm.at[:, pl.ds(g * split, split)], wq.at[:, pl.ds(g * split, split)], sems.at[3 + g]
        )
        for g in range(groups)
    ]
    wo_copy = pltpu.make_async_copy(wo_hbm, wo, sems.at[1])
    wh_copy = pltpu.make_async_copy(wh_hbm, wh, sems.at[2])
    gain_copy = pltpu.make_async_copy(gain_hbm, gain_ref, sems.at[5])
    head_gain_copy = pltpu.make_async_copy(head_gain_hbm, head_gain_ref, sems.at[6])
    bias_copy = pltpu.make_async_copy(bias_hbm, bias_ref, sems.at[7])
    for copy in [own_copy, gain_copy] + wq_copies + [wo_copy, head_gain_copy, wh_copy, bias_copy]:
        copy.start()
    core = core_ref[0]
    head = kv.shape[1] // 2
    half = own.shape[0]
    tokens = 2 * half
    start = 0
    for ref in kv_refs:
        kv[pl.ds(start, ref.shape[0]), :] = ref[...]
        start += ref.shape[0]
    length = start
    row = lax.broadcasted_iota(jnp.int32, (half, half), 0)
    col = lax.broadcasted_iota(jnp.int32, (half, half), 1)
    turn = jnp.where(row + col == half - 1, 1.0, 0.0).astype(BF16)
    second = jnp.where(
        core == 0,
        got_ref[0].astype(F32),
        jnp.dot(turn, passed_ref[...], preferred_element_type=F32),
    )
    first = jnp.dot(turn, mirrored_ref[...], preferred_element_type=F32)
    own_copy.wait()
    gain_copy.wait()
    first = jnp.where(core == 0, own[...].astype(F32), first)
    rows = jnp.concatenate([first, second], 0)
    normed = normalize(rows, gain_ref[...].astype(F32).reshape(1, -1))
    scale = 1.0 / math.sqrt(head)
    chunk = min(length, 1024)
    for number in range(heads):
        if number % (heads // groups) == 0:
            group = number // (heads // groups)
            at = group * split
            wq_copies[group].wait()
            queries[:, at : at + split] = jnp.dot(
                normed, wq[:, at : at + split], preferred_element_type=F32
            ).astype(BF16)
        query = queries[:, number * head : (number + 1) * head]

        def step(position, state):
            maxima, totals, summed = state
            at = pl.multiple_of(position * chunk, chunk)
            part = kv[pl.ds(at, chunk), :]
            scores = lax.dot_general(
                query, part[:, :head], (((1,), (1,)), ((), ())), preferred_element_type=F32
            )
            scores = jnp.where(scores == scores, scores * scale, -1e30)
            higher = jnp.maximum(maxima, jnp.max(scores, -1, keepdims=True))
            weights = jnp.exp(scores - higher)
            kept = jnp.exp(maxima - higher)
            totals = totals * kept + jnp.sum(weights, -1, keepdims=True)
            summed = summed * kept + jnp.dot(
                weights.astype(BF16), part[:, head:], preferred_element_type=F32
            )
            return higher, totals, summed

        state = (
            jnp.full((tokens, 1), -1e30, F32),
            jnp.zeros((tokens, 1), F32),
            jnp.zeros((tokens, head), F32),
        )
        if length == chunk:
            state = step(0, state)
        else:
            state = lax.fori_loop(0, length // chunk, step, state)
        attended[:, number * head : (number + 1) * head] = (state[2] / state[1]).astype(BF16)
    wo_copy.wait()
    head_gain_copy.wait()
    summed = rows + jnp.dot(attended[...], wo[...], preferred_element_type=F32)
    normed_out = normalize(summed, head_gain_ref[...].astype(F32).reshape(1, -1))
    wh_copy.wait()
    bias_copy.wait()
    tracks = wh.shape[1]
    width = 256
    bias = bias_ref[...].reshape(1, -1)
    for at in range(0, tracks, width):
        logits = jnp.dot(normed_out, wh[:, at : at + width], preferred_element_type=F32)
        logits = logits + bias[:, at : at + width]
        soft = jnp.maximum(logits, 0.0) + jnp.log1p(jnp.exp(-jnp.abs(logits)))
        predictions[:, at : at + width] = soft.astype(BF16)
    keep_ref[...] = predictions[pl.ds(pl.multiple_of(core * half, half), half), :]
    send_ref[...] = predictions[pl.ds(pl.multiple_of((1 - core) * half, half), half), :]


def transform(core, kvs, got, mirrored, passed, gain, head_gain, bias, own, wq, wo, wh):
    half, width = mirrored.shape
    tokens = 2 * half
    head = kvs[0].shape[1] // 2
    heads = wq.shape[1] // head
    length = sum(kv.shape[0] for kv in kvs)
    tracks = wh.shape[1]
    flops = 2 * tokens * (width * wq.shape[1] * 2 + width * tracks + 2 * length * wq.shape[1])
    return pl.pallas_call(
        functools.partial(block_kernel, len(kvs), heads),
        out_shape=(jax.ShapeDtypeStruct((half, tracks), BF16),) * 2,
        in_specs=[SMEM] + [VMEM] * (3 + len(kvs)) + [HBM] * 7,
        out_specs=(VMEM, VMEM),
        scratch_shapes=[
            pltpu.VMEM((half, width), BF16),
            pltpu.VMEM(gain.shape, BF16),
            pltpu.VMEM(wq.shape, BF16),
            pltpu.VMEM(wo.shape, BF16),
            pltpu.VMEM(head_gain.shape, BF16),
            pltpu.VMEM(wh.shape, BF16),
            pltpu.VMEM(bias.shape, F32),
            pltpu.VMEM((length, 2 * head), BF16),
            pltpu.VMEM((tokens, heads * head), BF16),
            pltpu.VMEM((tokens, heads * head), BF16),
            pltpu.VMEM((tokens, tracks), BF16),
            pltpu.SemaphoreType.DMA((8,)),
        ],
        compiler_params=pltpu.CompilerParams(vmem_limit_bytes=52 << 20),
        cost_estimate=pl.CostEstimate(
            flops=flops, bytes_accessed=2 * (wq.size + wo.size + wh.size), transcendentals=tokens * length * heads
        ),
        name="transform",
    )(core, *kvs, got, mirrored, passed, own, gain, wq, wo, head_gain, wh, bias)


def combine_kernel(core_ref, keep_ref, got_ref, perm_ref, out_ref):
    forward_here = core_ref[0] == 0
    tracks = perm_ref.shape[0]
    tokens = keep_ref.shape[0]
    order = perm_ref[...].reshape(1, -1)
    lanes = 128
    keep = keep_ref[...].astype(F32)
    got = got_ref[...].astype(F32)
    forward = jnp.where(forward_here, keep, got)
    reverse = jnp.where(forward_here, got, keep)
    for at in range(0, tracks, lanes):
        perm = jnp.broadcast_to(order[:, at : at + lanes], (tokens, lanes))
        within = perm & (lanes - 1)
        tile = perm >> 7
        picked = jnp.zeros((tokens, lanes), F32)
        for number in range(tracks // lanes):
            source = reverse[:, number * lanes : (number + 1) * lanes]
            found = jnp.take_along_axis(source, within, axis=1)
            picked = jnp.where(tile == number, found, picked)
        out_ref[:, at : at + lanes] = 0.5 * (forward[:, at : at + lanes] + picked)


def combine(core, keep, got, perm):
    return pl.pallas_call(
        combine_kernel,
        out_shape=jax.ShapeDtypeStruct(keep.shape, F32),
        in_specs=[SMEM] + [VMEM] * 3,
        out_specs=VMEM,
        compiler_params=pltpu.CompilerParams(vmem_limit_bytes=16 << 20),
        name="combine",
    )(core, keep, got, perm)


def gathered(kv):
    count = lax.axis_size("tok")
    if count > 16:
        mask = 2
        while mask < count:
            kv = jnp.concatenate([kv, exchange(kv, mask)], 0)
            mask *= 2
        return [kv]
    over_x = [exchange(kv, 2)] if count > 2 else []
    over_z = [exchange(kv, mask) for mask in range(count - 4, 0, -4)]
    return [kv] + over_x + over_z + [exchange(block, 2) for block in reversed(over_z)]


def per_device(
    hidden,
    base_ids,
    attn_gain,
    q_weight,
    kv_weight,
    out_weight,
    head_gain,
    head_weight,
    head_bias,
    track_perm,
):
    count = lax.axis_size("tok")
    core = (lax.axis_index("tok") & 1).astype(jnp.int32).reshape(1)
    got = exchange(hidden, 1)
    got_ids = exchange(base_ids, 1)
    mirrored = exchange(hidden[1], count - 2)
    kv = project(core, hidden, got, base_ids, got_ids, attn_gain, kv_weight)
    kvs = gathered(kv)
    passed = exchange(mirrored, 1)
    keep, send = transform(
        core,
        kvs,
        got,
        mirrored,
        passed,
        attn_gain,
        head_gain,
        head_bias,
        hidden,
        q_weight,
        out_weight,
        head_weight,
    )
    return combine(core, keep, exchange(send, 1), track_perm)


def solution(mesh):
    placed = (P("grp", "tok", None), P("grp", "tok"), P(), P(), P(), P(), P(), P(), P(), P())
    return jax.shard_map(
        per_device, mesh=mesh, in_specs=placed, out_specs=P(("grp", "tok"), None), check_vma=False
    )
```

```python
import functools
import math

import jax
import jax.numpy as jnp
from jax import lax
from jax.experimental import pallas as pl
from jax.experimental.pallas import tpu as pltpu
from jax.sharding import PartitionSpec as P

VMEM = pl.BlockSpec(memory_space=pltpu.VMEM)
SMEM = pl.BlockSpec(memory_space=pltpu.SMEM)
HBM = pl.BlockSpec(memory_space=pltpu.HBM)
ANY = pl.BlockSpec(memory_space=pl.ANY)
F32 = jnp.float32
BF16 = jnp.bfloat16


def in_hbm(value):
    return pltpu.with_memory_space_constraint(value, pltpu.HBM)


def exchange(value, mask):
    count = lax.axis_size("tok")
    return lax.ppermute(value, "tok", [(s, s ^ mask) for s in range(count)])


def normalize(rows, gain):
    mean = jnp.mean(rows * rows, -1, keepdims=True)
    return (rows * lax.rsqrt(mean + 1e-06) * gain).astype(BF16)


def fetch_kernel(places, *refs):
    *refs, sems = refs
    targets = refs[-len(places) :]
    copies = []
    for number, (argument, row) in enumerate(places):
        source = refs[argument] if row is None else refs[argument].at[row]
        copies.append(pltpu.make_async_copy(source, targets[number], sems.at[number]))
        copies[-1].start()
    for copy in copies:
        copy.wait()


def fetch(values, rows=(), after=None):
    places = [(number, None) for number in range(len(values))] + list(rows)
    shapes = [values[number].shape if row is None else values[number].shape[1:] for number, row in places]
    waited = [] if after is None else [after]
    return pl.pallas_call(
        functools.partial(fetch_kernel, places),
        out_shape=[
            jax.ShapeDtypeStruct(shape, values[number].dtype) for shape, (number, row) in zip(shapes, places)
        ],
        in_specs=[HBM] * len(values) + [ANY] * len(waited),
        out_specs=[VMEM] * len(places),
        scratch_shapes=[pltpu.SemaphoreType.DMA((len(places),))],
        compiler_params=pltpu.CompilerParams(vmem_limit_bytes=1 << 20),
        cost_estimate=pl.CostEstimate(
            flops=0, bytes_accessed=sum(2 * value.size for value in values), transcendentals=0
        ),
        name="fetch",
    )(*[in_hbm(value) for value in values], *waited)


def project_kernel(core_ref, got_ref, got_ids_ref, own_ref, own_ids_ref, gain_ref, weight_ref, kv_ref):
    core = core_ref[0]
    tokens = own_ref.shape[1]
    head = weight_ref.shape[1] // 2
    gain = gain_ref[...].astype(F32).reshape(1, -1)
    row = lax.broadcasted_iota(jnp.int32, (tokens, tokens), 0)
    col = lax.broadcasted_iota(jnp.int32, (tokens, tokens), 1)
    lane = lax.broadcasted_iota(jnp.int32, (tokens, weight_ref.shape[1]), 1)
    normed, left_out = [], []
    for ref, ids_ref in ((own_ref, own_ids_ref), (got_ref, got_ids_ref)):
        ids = jnp.where(core == 0, ids_ref[0:1, :], ids_ref[1:2, :])
        unknown = jnp.where((row == col) & (ids == 4), 1.0, 0.0)
        left_out.append((lane < head) & (jnp.max(unknown, -1, keepdims=True) > 0.5))
        normed.append(normalize(ref[core].astype(F32), gain))
    kv = jnp.dot(jnp.concatenate(normed, 0), weight_ref[...], preferred_element_type=F32)
    for part in range(2):
        kv_ref[pl.ds(part * tokens, tokens), :] = jnp.where(
            left_out[part], jnp.nan, kv[part * tokens : (part + 1) * tokens]
        ).astype(BF16)


def project(core, got, got_ids, own, own_ids, gain, weight):
    tokens, width = own.shape[1:]
    return pl.pallas_call(
        project_kernel,
        out_shape=jax.ShapeDtypeStruct((2 * tokens, weight.shape[1]), BF16),
        in_specs=[SMEM] + [VMEM] * 6,
        out_specs=VMEM,
        compiler_params=pltpu.CompilerParams(vmem_limit_bytes=12 << 20),
        cost_estimate=pl.CostEstimate(
            flops=4 * tokens * width * weight.shape[1], bytes_accessed=2 * weight.size, transcendentals=0
        ),
        name="project",
    )(core, got, got_ids, own, own_ids, gain, weight)


def turn_kernel(rows_ref, after_ref, turned_ref):
    tokens = rows_ref.shape[0]
    row = lax.broadcasted_iota(jnp.int32, (tokens, tokens), 0)
    col = lax.broadcasted_iota(jnp.int32, (tokens, tokens), 1)
    turn = jnp.where(row + col == tokens - 1, 1.0, 0.0).astype(BF16)
    turned_ref[...] = jnp.dot(turn, rows_ref[...], preferred_element_type=F32).astype(BF16)


def turned(rows, after):
    return pl.pallas_call(
        turn_kernel,
        out_shape=jax.ShapeDtypeStruct(rows.shape, BF16),
        in_specs=[VMEM, ANY],
        out_specs=VMEM,
        compiler_params=pltpu.CompilerParams(vmem_limit_bytes=4 << 20),
        name="turned",
    )(rows, after)


def query_kernel(core_ref, own_ref, got_ref, mirrored_ref, passed_ref, gain_ref, weight_ref, query_ref, rows_ref):
    core = core_ref[0]
    half = mirrored_ref.shape[0]
    head = query_ref.shape[1]
    rows_ref[pl.ds(0, half), :] = jnp.where(
        core == 0, own_ref[0].astype(F32), mirrored_ref[...].astype(F32)
    ).astype(BF16)
    rows_ref[pl.ds(half, half), :] = jnp.where(
        core == 0, got_ref[0].astype(F32), passed_ref[...].astype(F32)
    ).astype(BF16)
    normed = normalize(rows_ref[...].astype(F32), gain_ref[...].astype(F32).reshape(1, -1))
    queries = jnp.dot(normed, weight_ref[...], preferred_element_type=F32).astype(BF16)
    for number in range(weight_ref.shape[1] // head):
        query_ref[pl.ds(number * 2 * half, 2 * half), :] = queries[:, number * head : (number + 1) * head]


def query(core, own, got, mirrored, passed, gain, weight, head):
    half, width = mirrored.shape
    heads = weight.shape[1] // head
    return pl.pallas_call(
        query_kernel,
        out_shape=(
            jax.ShapeDtypeStruct((heads * 2 * half, head), BF16),
            jax.ShapeDtypeStruct((2 * half, width), BF16),
        ),
        in_specs=[SMEM] + [VMEM] * 6,
        out_specs=(VMEM, VMEM),
        compiler_params=pltpu.CompilerParams(vmem_limit_bytes=10 << 20),
        cost_estimate=pl.CostEstimate(
            flops=4 * half * width * weight.shape[1], bytes_accessed=2 * weight.size, transcendentals=0
        ),
        name="query",
    )(core, own, got, mirrored, passed, gain, weight)


def attend(queries, kv, length, state):
    head = queries.shape[1]
    rate = math.log2(math.e) / math.sqrt(head)
    chunk = min(length, 1024)

    def step(position, state):
        part = kv[pl.ds(pl.multiple_of(position * chunk, chunk), chunk), :]
        scores = lax.dot_general(
            queries, part[:, :head], (((1,), (1,)), ((), ())), preferred_element_type=F32
        )
        scores = jnp.where(scores == scores, scores, -1e30)
        maxima = jnp.max(scores, -1, keepdims=True)
        if state is not None:
            maxima = jnp.maximum(maxima, state[0])
        weights = jnp.exp2((scores - maxima) * rate)
        totals = jnp.sum(weights, -1, keepdims=True)
        summed = jnp.dot(weights.astype(BF16), part[:, head:], preferred_element_type=F32)
        if state is not None:
            kept = jnp.exp2((state[0] - maxima) * rate)
            totals = totals + state[1] * kept
            summed = summed + state[2] * kept
        return maxima, totals, summed

    state = step(0, state)
    if length > chunk:
        state = lax.fori_loop(1, length // chunk, step, state)
    return state


def pack(kv_refs, kv):
    start = 0
    for ref in kv_refs:
        kv[pl.ds(start, ref.shape[0]), :] = ref[...]
        start += ref.shape[0]
    return start


def first_kernel(heads, query_ref, *refs):
    *kv_refs, maxima_ref, totals_ref, summed_ref, kv = refs
    length = pack(kv_refs, kv)
    tokens = query_ref.shape[0] // heads
    for number in range(heads):
        at = pl.ds(number * tokens, tokens)
        maxima_ref[at, :], totals_ref[at, :], summed_ref[at, :] = attend(query_ref[at, :], kv, length, None)


def attention_cost(queries, kvs):
    length = sum(kv.shape[0] for kv in kvs)
    return 4 * queries.size * length, queries.shape[0] * length


def first_half(queries, kvs, heads):
    rows, head = queries.shape
    length = sum(kv.shape[0] for kv in kvs)
    flops, exponents = attention_cost(queries, kvs)
    return pl.pallas_call(
        functools.partial(first_kernel, heads),
        out_shape=(
            jax.ShapeDtypeStruct((rows, 1), F32),
            jax.ShapeDtypeStruct((rows, 1), F32),
            jax.ShapeDtypeStruct((rows, head), F32),
        ),
        in_specs=[VMEM] * (1 + len(kvs)),
        out_specs=(VMEM,) * 3,
        scratch_shapes=[pltpu.VMEM((length, 2 * head), BF16)],
        compiler_params=pltpu.CompilerParams(vmem_limit_bytes=12 << 20),
        cost_estimate=pl.CostEstimate(flops=flops, bytes_accessed=queries.size, transcendentals=exponents),
        name="first_half",
    )(queries, *kvs)


def block_kernel(count, heads, core_ref, query_ref, rows_ref, *refs):
    kv_refs = refs[:count]
    *state_refs, wo, head_gain_ref, wh, bias_ref, keep_ref, send_ref, kv, attended, predictions = refs[count:]
    core = core_ref[0]
    tokens = rows_ref.shape[0]
    half = tokens // 2
    head = query_ref.shape[1]
    length = pack(kv_refs, kv)
    for number in range(heads):
        at = pl.ds(number * tokens, tokens)
        state = tuple(ref[at, :] for ref in state_refs) or None
        _, totals, summed = attend(query_ref[at, :], kv, length, state)
        attended[:, number * head : (number + 1) * head] = (summed / totals).astype(BF16)
    summed = rows_ref[...].astype(F32) + jnp.dot(attended[...], wo[...], preferred_element_type=F32)
    normed_out = normalize(summed, head_gain_ref[...].astype(F32).reshape(1, -1))
    tracks = wh.shape[1]
    width = 256
    bias = bias_ref[...].reshape(1, -1)
    for at in range(0, tracks, width):
        logits = jnp.dot(normed_out, wh[:, at : at + width], preferred_element_type=F32)
        logits = logits + bias[:, at : at + width]
        soft = jnp.maximum(logits, 0.0) + jnp.log1p(jnp.exp(-jnp.abs(logits)))
        predictions[:, at : at + width] = soft.astype(BF16)
    keep_ref[...] = predictions[pl.ds(pl.multiple_of(core * half, half), half), :]
    send_ref[...] = predictions[pl.ds(pl.multiple_of((1 - core) * half, half), half), :]


def transform(core, queries, rows, kvs, state, wo, head_gain, wh, bias):
    tokens, _ = rows.shape
    head = queries.shape[1]
    heads = queries.shape[0] // tokens
    length = sum(kv.shape[0] for kv in kvs)
    tracks = wh.shape[1]
    flops, exponents = attention_cost(queries, kvs)
    return pl.pallas_call(
        functools.partial(block_kernel, len(kvs), heads),
        out_shape=(jax.ShapeDtypeStruct((tokens // 2, tracks), BF16),) * 2,
        in_specs=[SMEM] + [VMEM] * (6 + len(kvs) + len(state)),
        out_specs=(VMEM, VMEM),
        scratch_shapes=[
            pltpu.VMEM((length, 2 * head), BF16),
            pltpu.VMEM((tokens, heads * head), BF16),
            pltpu.VMEM((tokens, tracks), BF16),
        ],
        compiler_params=pltpu.CompilerParams(vmem_limit_bytes=28 << 20),
        cost_estimate=pl.CostEstimate(
            flops=flops + 2 * tokens * (wo.size + wh.size),
            bytes_accessed=2 * (wo.size + wh.size),
            transcendentals=exponents,
        ),
        name="transform",
    )(core, queries, rows, *kvs, *state, wo, head_gain, wh, bias)


def combine_kernel(core_ref, keep_ref, got_ref, perm_ref, out_ref):
    forward_here = core_ref[0] == 0
    tracks = perm_ref.shape[0]
    tokens = keep_ref.shape[0]
    order = perm_ref[...].reshape(1, -1)
    lanes = 128
    keep = keep_ref[...].astype(F32)
    got = got_ref[...].astype(F32)
    forward = jnp.where(forward_here, keep, got)
    reverse = jnp.where(forward_here, got, keep)
    for at in range(0, tracks, lanes):
        perm = jnp.broadcast_to(order[:, at : at + lanes], (tokens, lanes))
        within = perm & (lanes - 1)
        tile = perm >> 7
        picked = jnp.zeros((tokens, lanes), F32)
        for number in range(tracks // lanes):
            source = reverse[:, number * lanes : (number + 1) * lanes]
            found = jnp.take_along_axis(source, within, axis=1)
            picked = jnp.where(tile == number, found, picked)
        out_ref[:, at : at + lanes] = 0.5 * (forward[:, at : at + lanes] + picked)


def combine(core, keep, got, perm):
    return pl.pallas_call(
        combine_kernel,
        out_shape=jax.ShapeDtypeStruct(keep.shape, F32),
        in_specs=[SMEM] + [VMEM] * 3,
        out_specs=VMEM,
        compiler_params=pltpu.CompilerParams(vmem_limit_bytes=16 << 20),
        name="combine",
    )(core, keep, got, perm)


def gathered(kv):
    count = lax.axis_size("tok")
    if count != 16:
        mask = 2
        while mask < count:
            kv = jnp.concatenate([kv, exchange(kv, mask)], 0)
            mask *= 2
        return [], [kv]
    z2 = exchange(kv, 8)
    z1 = exchange(kv, 4)
    x = exchange(kv, 2)
    xz1 = exchange(z1, 2)
    z3 = exchange(z2, 4)
    xz2 = exchange(z2, 2)
    xz3 = exchange(z3, 2)
    return [kv, z1, x, z2], [xz1, z3, xz2, xz3]


def per_device(
    hidden,
    base_ids,
    attn_gain,
    q_weight,
    kv_weight,
    out_weight,
    head_gain,
    head_weight,
    head_bias,
    track_perm,
):
    count = lax.axis_size("tok")
    core = (lax.axis_index("tok") & 1).astype(jnp.int32).reshape(1)
    got = exchange(hidden, 1)
    got_ids = exchange(base_ids, 1)
    own, gain, own_ids, kv_weight, reverse = fetch([hidden, attn_gain, base_ids, kv_weight], [(0, 1)])
    mirrored = exchange(reverse, count - 2)
    kv = project(core, got, got_ids, own, own_ids, gain, kv_weight)
    early, late = gathered(kv)
    wq, wo, head_gain, wh, bias = fetch([q_weight, out_weight, head_gain, head_weight, head_bias], after=kv)
    mirrored = turned(mirrored, early[-1] if early else kv)
    passed = exchange(mirrored, 1)
    head = kv.shape[1] // 2
    queries, rows = query(core, own, got, mirrored, passed, gain, wq, head)
    state = ()
    if early:
        state = first_half(queries, early, wq.shape[1] // head)
    keep, send = transform(core, queries, rows, late, state, wo, head_gain, wh, bias)
    return combine(core, keep, exchange(send, 1), track_perm)


def solution(mesh):
    placed = (P("grp", "tok", None), P("grp", "tok"), P(), P(), P(), P(), P(), P(), P(), P())
    return jax.shard_map(per_device, mesh=mesh, in_specs=placed, out_specs=P(("grp", "tok"), None), check_vma=False)
```

```python
import functools
import math

import jax
import jax.numpy as jnp
from jax import lax
from jax.experimental import pallas as pl
from jax.experimental.pallas import tpu as pltpu
from jax.sharding import PartitionSpec as P

VMEM = pl.BlockSpec(memory_space=pltpu.VMEM)
SMEM = pl.BlockSpec(memory_space=pltpu.SMEM)
HBM = pl.BlockSpec(memory_space=pltpu.HBM)
ANY = pl.BlockSpec(memory_space=pl.ANY)
F32 = jnp.float32
BF16 = jnp.bfloat16


def in_hbm(value):
    return pltpu.with_memory_space_constraint(value, pltpu.HBM)


def exchange(value, mask):
    count = lax.axis_size("tok")
    return lax.ppermute(value, "tok", [(s, s ^ mask) for s in range(count)])


def normalize(rows, gain):
    mean = jnp.mean(rows * rows, -1, keepdims=True)
    return (rows * lax.rsqrt(mean + 1e-06) * gain).astype(BF16)


def fetch_kernel(places, *refs):
    *refs, sems = refs
    targets = refs[-len(places) :]
    copies = []
    for number, (argument, row) in enumerate(places):
        source = refs[argument] if row is None else refs[argument].at[row]
        copies.append(pltpu.make_async_copy(source, targets[number], sems.at[number]))
        copies[-1].start()
    for copy in copies:
        copy.wait()


def fetch(values, rows=(), after=None):
    places = [(number, None) for number in range(len(values))] + list(rows)
    shapes = [values[number].shape if row is None else values[number].shape[1:] for number, row in places]
    waited = [] if after is None else [after]
    return pl.pallas_call(
        functools.partial(fetch_kernel, places),
        out_shape=[
            jax.ShapeDtypeStruct(shape, values[number].dtype) for shape, (number, row) in zip(shapes, places)
        ],
        in_specs=[HBM] * len(values) + [ANY] * len(waited),
        out_specs=[VMEM] * len(places),
        scratch_shapes=[pltpu.SemaphoreType.DMA((len(places),))],
        compiler_params=pltpu.CompilerParams(vmem_limit_bytes=1 << 20),
        cost_estimate=pl.CostEstimate(
            flops=0, bytes_accessed=sum(2 * value.size for value in values), transcendentals=0
        ),
        name="fetch",
    )(*[in_hbm(value) for value in values], *waited)


def project_kernel(core_ref, got_ref, got_ids_ref, own_ref, own_ids_ref, gain_ref, weight_ref, kv_ref):
    core = core_ref[0]
    tokens = own_ref.shape[1]
    head = weight_ref.shape[1] // 2
    gain = gain_ref[...].astype(F32).reshape(1, -1)
    row = lax.broadcasted_iota(jnp.int32, (tokens, tokens), 0)
    col = lax.broadcasted_iota(jnp.int32, (tokens, tokens), 1)
    lane = lax.broadcasted_iota(jnp.int32, (tokens, weight_ref.shape[1]), 1)
    normed, left_out = [], []
    for ref, ids_ref in ((own_ref, own_ids_ref), (got_ref, got_ids_ref)):
        ids = jnp.where(core == 0, ids_ref[0:1, :], ids_ref[1:2, :])
        unknown = jnp.where((row == col) & (ids == 4), 1.0, 0.0)
        left_out.append((lane < head) & (jnp.max(unknown, -1, keepdims=True) > 0.5))
        normed.append(normalize(ref[core].astype(F32), gain))
    kv = jnp.dot(jnp.concatenate(normed, 0), weight_ref[...], preferred_element_type=F32)
    for part in range(2):
        kv_ref[pl.ds(part * tokens, tokens), :] = jnp.where(
            left_out[part], jnp.nan, kv[part * tokens : (part + 1) * tokens]
        ).astype(BF16)


def project(core, got, got_ids, own, own_ids, gain, weight):
    tokens, width = own.shape[1:]
    return pl.pallas_call(
        project_kernel,
        out_shape=jax.ShapeDtypeStruct((2 * tokens, weight.shape[1]), BF16),
        in_specs=[SMEM] + [VMEM] * 6,
        out_specs=VMEM,
        compiler_params=pltpu.CompilerParams(vmem_limit_bytes=12 << 20),
        cost_estimate=pl.CostEstimate(
            flops=4 * tokens * width * weight.shape[1], bytes_accessed=2 * weight.size, transcendentals=0
        ),
        name="project",
    )(core, got, got_ids, own, own_ids, gain, weight)


def turn_kernel(rows_ref, after_ref, turned_ref):
    tokens = rows_ref.shape[0]
    row = lax.broadcasted_iota(jnp.int32, (tokens, tokens), 0)
    col = lax.broadcasted_iota(jnp.int32, (tokens, tokens), 1)
    turn = jnp.where(row + col == tokens - 1, 1.0, 0.0).astype(BF16)
    turned_ref[...] = jnp.dot(turn, rows_ref[...], preferred_element_type=F32).astype(BF16)


def turned(rows, after):
    return pl.pallas_call(
        turn_kernel,
        out_shape=jax.ShapeDtypeStruct(rows.shape, BF16),
        in_specs=[VMEM, ANY],
        out_specs=VMEM,
        compiler_params=pltpu.CompilerParams(vmem_limit_bytes=4 << 20),
        name="turned",
    )(rows, after)


def attend(queries, kv, length, state):
    head = queries.shape[1]
    rate = math.log2(math.e) / math.sqrt(head)
    chunk = min(length, 1024)

    def step(position, state):
        part = kv[pl.ds(pl.multiple_of(position * chunk, chunk), chunk), :]
        scores = lax.dot_general(
            queries, part[:, :head], (((1,), (1,)), ((), ())), preferred_element_type=F32
        )
        scores = jnp.where(scores == scores, scores, -1e30)
        maxima = jnp.max(scores, -1, keepdims=True)
        if state is not None:
            maxima = jnp.maximum(maxima, state[0])
        weights = jnp.exp2((scores - maxima) * rate)
        totals = jnp.sum(weights, -1, keepdims=True)
        summed = jnp.dot(weights.astype(BF16), part[:, head:], preferred_element_type=F32)
        if state is not None:
            kept = jnp.exp2((state[0] - maxima) * rate)
            totals = totals + state[1] * kept
            summed = summed + state[2] * kept
        return maxima, totals, summed

    state = step(0, state)
    if length > chunk:
        state = lax.fori_loop(1, length // chunk, step, state)
    return state


def pack(kv_refs, kv):
    start = 0
    for ref in kv_refs:
        kv[pl.ds(start, ref.shape[0]), :] = ref[...]
        start += ref.shape[0]
    return start


def block_kernel(count, core_ref, own_ref, got_ref, mirrored_ref, passed_ref, *refs):
    kv_refs = refs[:count]
    gain_ref, wq, wo, head_gain_ref, wh, bias_ref, keep_ref, send_ref = refs[count : count + 8]
    kv, attended, predictions = refs[count + 8 :]
    core = core_ref[0]
    half = mirrored_ref.shape[0]
    head = kv.shape[1] // 2
    length = pack(kv_refs, kv)
    first = jnp.where(core == 0, own_ref[0].astype(F32), mirrored_ref[...].astype(F32))
    second = jnp.where(core == 0, got_ref[0].astype(F32), passed_ref[...].astype(F32))
    rows = jnp.concatenate([first, second], 0)
    normed = normalize(rows, gain_ref[...].astype(F32).reshape(1, -1))
    queries = jnp.dot(normed, wq[...], preferred_element_type=F32).astype(BF16)
    for at in range(0, wq.shape[1], head):
        _, totals, summed = attend(queries[:, at : at + head], kv, length, None)
        attended[:, at : at + head] = (summed / totals).astype(BF16)
    summed = rows + jnp.dot(attended[...], wo[...], preferred_element_type=F32)
    normed_out = normalize(summed, head_gain_ref[...].astype(F32).reshape(1, -1))
    tracks = wh.shape[1]
    width = 256
    bias = bias_ref[...].reshape(1, -1)
    for at in range(0, tracks, width):
        logits = jnp.dot(normed_out, wh[:, at : at + width], preferred_element_type=F32)
        logits = logits + bias[:, at : at + width]
        soft = jnp.maximum(logits, 0.0) + jnp.log1p(jnp.exp(-jnp.abs(logits)))
        predictions[:, at : at + width] = soft.astype(BF16)
    keep_ref[...] = predictions[pl.ds(pl.multiple_of(core * half, half), half), :]
    send_ref[...] = predictions[pl.ds(pl.multiple_of((1 - core) * half, half), half), :]


def transform(core, own, got, mirrored, passed, kvs, gain, wq, wo, head_gain, wh, bias):
    half, width = mirrored.shape
    tokens = 2 * half
    length = sum(kv.shape[0] for kv in kvs)
    tracks = wh.shape[1]
    flops = 2 * tokens * (width * wq.shape[1] * 2 + width * tracks + 2 * length * wq.shape[1])
    return pl.pallas_call(
        functools.partial(block_kernel, len(kvs)),
        out_shape=(jax.ShapeDtypeStruct((half, tracks), BF16),) * 2,
        in_specs=[SMEM] + [VMEM] * (10 + len(kvs)),
        out_specs=(VMEM, VMEM),
        scratch_shapes=[
            pltpu.VMEM((length, kvs[0].shape[1]), BF16),
            pltpu.VMEM((tokens, wq.shape[1]), BF16),
            pltpu.VMEM((tokens, tracks), BF16),
        ],
        compiler_params=pltpu.CompilerParams(vmem_limit_bytes=28 << 20),
        cost_estimate=pl.CostEstimate(
            flops=flops,
            bytes_accessed=2 * (wq.size + wo.size + wh.size),
            transcendentals=tokens * length * wq.shape[1] * 2 // kvs[0].shape[1],
        ),
        name="transform",
    )(core, own, got, mirrored, passed, *kvs, gain, wq, wo, head_gain, wh, bias)


def combine_kernel(core_ref, keep_ref, got_ref, perm_ref, out_ref):
    forward_here = core_ref[0] == 0
    tracks = perm_ref.shape[0]
    tokens = keep_ref.shape[0]
    order = perm_ref[...].reshape(1, -1)
    lanes = 128
    keep = keep_ref[...].astype(F32)
    got = got_ref[...].astype(F32)
    forward = jnp.where(forward_here, keep, got)
    reverse = jnp.where(forward_here, got, keep)
    for at in range(0, tracks, lanes):
        perm = jnp.broadcast_to(order[:, at : at + lanes], (tokens, lanes))
        within = perm & (lanes - 1)
        tile = perm >> 7
        picked = jnp.zeros((tokens, lanes), F32)
        for number in range(tracks // lanes):
            source = reverse[:, number * lanes : (number + 1) * lanes]
            found = jnp.take_along_axis(source, within, axis=1)
            picked = jnp.where(tile == number, found, picked)
        out_ref[:, at : at + lanes] = 0.5 * (forward[:, at : at + lanes] + picked)


def combine(core, keep, got, perm):
    return pl.pallas_call(
        combine_kernel,
        out_shape=jax.ShapeDtypeStruct(keep.shape, F32),
        in_specs=[SMEM] + [VMEM] * 3,
        out_specs=VMEM,
        compiler_params=pltpu.CompilerParams(vmem_limit_bytes=16 << 20),
        name="combine",
    )(core, keep, got, perm)


def gathered(kv):
    count = lax.axis_size("tok")
    if count != 16:
        mask = 2
        while mask < count:
            kv = jnp.concatenate([kv, exchange(kv, mask)], 0)
            mask *= 2
        return [kv], kv
    z2 = exchange(kv, 8)
    z1 = exchange(kv, 4)
    x = exchange(kv, 2)
    xz1 = exchange(z1, 2)
    z3 = exchange(z2, 4)
    xz2 = exchange(z2, 2)
    xz3 = exchange(z3, 2)
    return [kv, x, z1, xz1, z2, xz2, z3, xz3], z2


def per_device(
    hidden,
    base_ids,
    attn_gain,
    q_weight,
    kv_weight,
    out_weight,
    head_gain,
    head_weight,
    head_bias,
    track_perm,
):
    count = lax.axis_size("tok")
    core = (lax.axis_index("tok") & 1).astype(jnp.int32).reshape(1)
    got = exchange(hidden, 1)
    got_ids = exchange(base_ids, 1)
    own, gain, own_ids, kv_weight, reverse = fetch([hidden, attn_gain, base_ids, kv_weight], [(0, 1)])
    mirrored = exchange(reverse, count - 2)
    kv = project(core, got, got_ids, own, own_ids, gain, kv_weight)
    kvs, _ = gathered(kv)
    wh, bias = fetch([head_weight, head_bias], after=kv)
    wq, wo, head_gain = fetch([q_weight, out_weight, head_gain], after=bias)
    mirrored = turned(mirrored, head_gain)
    passed = exchange(mirrored, 1)
    keep, send = transform(core, own, got, mirrored, passed, kvs, gain, wq, wo, head_gain, wh, bias)
    return combine(core, keep, exchange(send, 1), track_perm)


def solution(mesh):
    placed = (P("grp", "tok", None), P("grp", "tok"), P(), P(), P(), P(), P(), P(), P(), P())
    return jax.shard_map(
        per_device, mesh=mesh, in_specs=placed, out_specs=P(("grp", "tok"), None), check_vma=False
    )
```

```python
import functools
import math

import jax
import jax.numpy as jnp
from jax import lax
from jax.experimental import pallas as pl
from jax.experimental.pallas import tpu as pltpu
from jax.sharding import PartitionSpec as P

VMEM = pl.BlockSpec(memory_space=pltpu.VMEM)
SMEM = pl.BlockSpec(memory_space=pltpu.SMEM)
HBM = pl.BlockSpec(memory_space=pltpu.HBM)
ANY = pl.BlockSpec(memory_space=pl.ANY)
F32 = jnp.float32
BF16 = jnp.bfloat16


def in_hbm(value):
    return pltpu.with_memory_space_constraint(value, pltpu.HBM)


def exchange(value, mask):
    count = lax.axis_size("tok")
    return lax.ppermute(value, "tok", [(s, s ^ mask) for s in range(count)])


def normalize(rows, gain):
    mean = jnp.mean(rows * rows, -1, keepdims=True)
    return (rows * lax.rsqrt(mean + 1e-06) * gain).astype(BF16)


def fetch_kernel(places, *refs):
    *refs, sems = refs
    targets = refs[-len(places) :]
    copies = []
    for number, (argument, row) in enumerate(places):
        source = refs[argument] if row is None else refs[argument].at[row]
        copies.append(pltpu.make_async_copy(source, targets[number], sems.at[number]))
        copies[-1].start()
    for copy in copies:
        copy.wait()


def fetch(values, rows=(), after=None):
    places = [(number, None) for number in range(len(values))] + list(rows)
    shapes = [values[number].shape if row is None else values[number].shape[1:] for number, row in places]
    waited = [] if after is None else [after]
    return pl.pallas_call(
        functools.partial(fetch_kernel, places),
        out_shape=[
            jax.ShapeDtypeStruct(shape, values[number].dtype) for shape, (number, row) in zip(shapes, places)
        ],
        in_specs=[HBM] * len(values) + [ANY] * len(waited),
        out_specs=[VMEM] * len(places),
        scratch_shapes=[pltpu.SemaphoreType.DMA((len(places),))],
        compiler_params=pltpu.CompilerParams(vmem_limit_bytes=1 << 20),
        cost_estimate=pl.CostEstimate(
            flops=0, bytes_accessed=sum(2 * value.size for value in values), transcendentals=0
        ),
        name="fetch",
    )(*[in_hbm(value) for value in values], *waited)


def project_kernel(core_ref, got_ref, got_ids_ref, own_ref, own_ids_ref, gain_ref, weight_ref, kv_ref):
    core = core_ref[0]
    tokens = own_ref.shape[1]
    head = weight_ref.shape[1] // 2
    gain = gain_ref[...].astype(F32).reshape(1, -1)
    row = lax.broadcasted_iota(jnp.int32, (tokens, tokens), 0)
    col = lax.broadcasted_iota(jnp.int32, (tokens, tokens), 1)
    lane = lax.broadcasted_iota(jnp.int32, (tokens, weight_ref.shape[1]), 1)
    normed, left_out = [], []
    for ref, ids_ref in ((own_ref, own_ids_ref), (got_ref, got_ids_ref)):
        ids = jnp.where(core == 0, ids_ref[0:1, :], ids_ref[1:2, :])
        unknown = jnp.where((row == col) & (ids == 4), 1.0, 0.0)
        left_out.append((lane < head) & (jnp.max(unknown, -1, keepdims=True) > 0.5))
        normed.append(normalize(ref[core].astype(F32), gain))
    kv = jnp.dot(jnp.concatenate(normed, 0), weight_ref[...], preferred_element_type=F32)
    for part in range(2):
        kv_ref[pl.ds(part * tokens, tokens), :] = jnp.where(
            left_out[part], jnp.nan, kv[part * tokens : (part + 1) * tokens]
        ).astype(BF16)


def project(core, got, got_ids, own, own_ids, gain, weight):
    tokens, width = own.shape[1:]
    return pl.pallas_call(
        project_kernel,
        out_shape=jax.ShapeDtypeStruct((2 * tokens, weight.shape[1]), BF16),
        in_specs=[SMEM] + [VMEM] * 6,
        out_specs=VMEM,
        compiler_params=pltpu.CompilerParams(vmem_limit_bytes=12 << 20),
        cost_estimate=pl.CostEstimate(
            flops=4 * tokens * width * weight.shape[1], bytes_accessed=2 * weight.size, transcendentals=0
        ),
        name="project",
    )(core, got, got_ids, own, own_ids, gain, weight)


def turn_kernel(rows_ref, after_ref, turned_ref):
    tokens = rows_ref.shape[0]
    row = lax.broadcasted_iota(jnp.int32, (tokens, tokens), 0)
    col = lax.broadcasted_iota(jnp.int32, (tokens, tokens), 1)
    turn = jnp.where(row + col == tokens - 1, 1.0, 0.0).astype(BF16)
    turned_ref[...] = jnp.dot(turn, rows_ref[...], preferred_element_type=F32).astype(BF16)


def turned(rows, after):
    return pl.pallas_call(
        turn_kernel,
        out_shape=jax.ShapeDtypeStruct(rows.shape, BF16),
        in_specs=[VMEM, ANY],
        out_specs=VMEM,
        compiler_params=pltpu.CompilerParams(vmem_limit_bytes=4 << 20),
        name="turned",
    )(rows, after)


def attend(queries, kv, length, state):
    head = queries.shape[1]
    rate = math.log2(math.e) / math.sqrt(head)
    chunk = min(length, 1024)

    def step(position, state):
        part = kv[pl.ds(pl.multiple_of(position * chunk, chunk), chunk), :]
        scores = lax.dot_general(
            queries, part[:, :head], (((1,), (1,)), ((), ())), preferred_element_type=F32
        )
        scores = jnp.where(scores == scores, scores, -1e30)
        maxima = jnp.max(scores, -1, keepdims=True)
        if state is not None:
            maxima = jnp.maximum(maxima, state[0])
        weights = jnp.exp2((scores - maxima) * rate)
        totals = jnp.sum(weights, -1, keepdims=True)
        summed = jnp.dot(weights.astype(BF16), part[:, head:], preferred_element_type=F32)
        if state is not None:
            kept = jnp.exp2((state[0] - maxima) * rate)
            totals = totals + state[1] * kept
            summed = summed + state[2] * kept
        return maxima, totals, summed

    state = step(0, state)
    if length > chunk:
        state = lax.fori_loop(1, length // chunk, step, state)
    return state


def pack(kv_refs, kv):
    start = 0
    for ref in kv_refs:
        kv[pl.ds(start, ref.shape[0]), :] = ref[...]
        start += ref.shape[0]
    return start


def query_kernel(core_ref, own_ref, got_ref, mirrored_ref, passed_ref, gain_ref, weight_ref, query_ref, rows_ref):
    core = core_ref[0]
    half = mirrored_ref.shape[0]
    head = query_ref.shape[1]
    first = jnp.where(core == 0, own_ref[0].astype(F32), mirrored_ref[...].astype(F32))
    second = jnp.where(core == 0, got_ref[0].astype(F32), passed_ref[...].astype(F32))
    rows = jnp.concatenate([first, second], 0)
    rows_ref[...] = rows
    normed = normalize(rows, gain_ref[...].astype(F32).reshape(1, -1))
    queries = jnp.dot(normed, weight_ref[...], preferred_element_type=F32).astype(BF16)
    for number in range(weight_ref.shape[1] // head):
        query_ref[pl.ds(number * 2 * half, 2 * half), :] = queries[:, number * head : (number + 1) * head]


def query(core, own, got, mirrored, passed, gain, weight, head):
    half, width = mirrored.shape
    heads = weight.shape[1] // head
    return pl.pallas_call(
        query_kernel,
        out_shape=(
            jax.ShapeDtypeStruct((heads * 2 * half, head), BF16),
            jax.ShapeDtypeStruct((2 * half, width), F32),
        ),
        in_specs=[SMEM] + [VMEM] * 6,
        out_specs=(VMEM, VMEM),
        compiler_params=pltpu.CompilerParams(vmem_limit_bytes=10 << 20),
        cost_estimate=pl.CostEstimate(
            flops=4 * half * width * weight.shape[1], bytes_accessed=2 * weight.size, transcendentals=0
        ),
        name="query",
    )(core, own, got, mirrored, passed, gain, weight)


def block_kernel(count, core_ref, query_ref, rows_ref, *refs):
    kv_refs = refs[:count]
    wo, head_gain_ref, wh, bias_ref, keep_ref, send_ref = refs[count : count + 6]
    kv, attended, predictions = refs[count + 6 :]
    core = core_ref[0]
    tokens = rows_ref.shape[0]
    half = tokens // 2
    head = query_ref.shape[1]
    length = pack(kv_refs, kv)
    _, totals, summed = attend(query_ref[...], kv, length, None)
    result = (summed / totals).astype(BF16)
    for number in range(query_ref.shape[0] // tokens):
        attended[:, number * head : (number + 1) * head] = result[number * tokens : (number + 1) * tokens]
    summed = rows_ref[...] + jnp.dot(attended[...], wo[...], preferred_element_type=F32)
    normed_out = normalize(summed, head_gain_ref[...].astype(F32).reshape(1, -1))
    tracks = wh.shape[1]
    width = 256
    bias = bias_ref[...].reshape(1, -1)
    for at in range(0, tracks, width):
        logits = jnp.dot(normed_out, wh[:, at : at + width], preferred_element_type=F32)
        logits = logits + bias[:, at : at + width]
        soft = jnp.maximum(logits, 0.0) + jnp.log1p(jnp.exp(-jnp.abs(logits)))
        predictions[:, at : at + width] = soft.astype(BF16)
    keep_ref[...] = predictions[pl.ds(pl.multiple_of(core * half, half), half), :]
    send_ref[...] = predictions[pl.ds(pl.multiple_of((1 - core) * half, half), half), :]


def transform(core, queries, rows, kvs, wo, head_gain, wh, bias):
    tokens, _ = rows.shape
    head = queries.shape[1]
    length = sum(kv.shape[0] for kv in kvs)
    tracks = wh.shape[1]
    return pl.pallas_call(
        functools.partial(block_kernel, len(kvs)),
        out_shape=(jax.ShapeDtypeStruct((tokens // 2, tracks), BF16),) * 2,
        in_specs=[SMEM] + [VMEM] * (6 + len(kvs)),
        out_specs=(VMEM, VMEM),
        scratch_shapes=[
            pltpu.VMEM((length, 2 * head), BF16),
            pltpu.VMEM((tokens, wo.shape[0]), BF16),
            pltpu.VMEM((tokens, tracks), BF16),
        ],
        compiler_params=pltpu.CompilerParams(vmem_limit_bytes=28 << 20),
        cost_estimate=pl.CostEstimate(
            flops=2 * tokens * (wo.size + wh.size) + 4 * queries.size * length,
            bytes_accessed=2 * (wo.size + wh.size),
            transcendentals=queries.shape[0] * length,
        ),
        name="transform",
    )(core, queries, rows, *kvs, wo, head_gain, wh, bias)


def combine_kernel(core_ref, keep_ref, got_ref, perm_ref, out_ref, forward_ref, reverse_ref):
    forward_here = core_ref[0] == 0
    keep = keep_ref[...].astype(F32)
    got = got_ref[...].astype(F32)
    forward_ref[...] = jnp.where(forward_here, keep, got)
    reverse_ref[...] = jnp.where(forward_here, got, keep)
    tracks = perm_ref.shape[0]
    tokens = keep_ref.shape[0]
    order = perm_ref[...].reshape(1, -1)
    lanes = 128
    group = 8
    for at in range(0, tracks, lanes):
        perm = jnp.broadcast_to(order[:, at : at + lanes], (group, lanes))
        within = perm & (lanes - 1)
        tile = perm >> 7
        inside = [tile == number for number in range(1, tracks // lanes)]
        for row in range(0, tokens, group):
            rows = slice(row, row + group)
            picked = jnp.take_along_axis(reverse_ref[rows, :lanes], within, axis=1)
            for number, here in enumerate(inside, 1):
                source = reverse_ref[rows, number * lanes : (number + 1) * lanes]
                picked = jnp.where(here, jnp.take_along_axis(source, within, axis=1), picked)
            out_ref[rows, at : at + lanes] = 0.5 * (forward_ref[rows, at : at + lanes] + picked)


def combine(core, keep, got, perm):
    return pl.pallas_call(
        combine_kernel,
        out_shape=jax.ShapeDtypeStruct(keep.shape, F32),
        in_specs=[SMEM] + [VMEM] * 3,
        out_specs=VMEM,
        scratch_shapes=[pltpu.VMEM(keep.shape, F32)] * 2,
        compiler_params=pltpu.CompilerParams(vmem_limit_bytes=16 << 20),
        name="combine",
    )(core, keep, got, perm)


def gathered(kv):
    count = lax.axis_size("tok")
    if count != 16:
        mask = 2
        while mask < count:
            kv = jnp.concatenate([kv, exchange(kv, mask)], 0)
            mask *= 2
        return [kv], kv
    z2 = exchange(kv, 8)
    z1 = exchange(kv, 4)
    x = exchange(kv, 2)
    xz1 = exchange(z1, 2)
    z3 = exchange(z2, 4)
    xz2 = exchange(z2, 2)
    xz3 = exchange(z3, 2)
    return [kv, x, z1, xz1, z2, xz2, z3, xz3], z2


def per_device(
    hidden,
    base_ids,
    attn_gain,
    q_weight,
    kv_weight,
    out_weight,
    head_gain,
    head_weight,
    head_bias,
    track_perm,
):
    count = lax.axis_size("tok")
    core = (lax.axis_index("tok") & 1).astype(jnp.int32).reshape(1)
    got = exchange(hidden, 1)
    got_ids = exchange(base_ids, 1)
    own, gain, own_ids, kv_weight, reverse = fetch([hidden, attn_gain, base_ids, kv_weight], [(0, 1)])
    mirrored = exchange(reverse, count - 2)
    kv = project(core, got, got_ids, own, own_ids, gain, kv_weight)
    kvs, _ = gathered(kv)
    wh, bias = fetch([head_weight, head_bias], after=kv)
    wq, wo, head_gain = fetch([q_weight, out_weight, head_gain], after=bias)
    mirrored = turned(mirrored, head_gain)
    passed = exchange(mirrored, 1)
    queries, rows = query(core, own, got, mirrored, passed, gain, wq, kv.shape[1] // 2)
    keep, send = transform(core, queries, rows, kvs, wo, head_gain, wh, bias)
    return combine(core, keep, exchange(send, 1), track_perm)


def solution(mesh):
    placed = (P("grp", "tok", None), P("grp", "tok"), P(), P(), P(), P(), P(), P(), P(), P())
    return jax.shard_map(per_device, mesh=mesh, in_specs=placed, out_specs=P(("grp", "tok"), None), check_vma=False)
```

```python
import functools
import math

import jax
import jax.numpy as jnp
from jax import lax
from jax.experimental import pallas as pl
from jax.experimental.pallas import tpu as pltpu
from jax.sharding import PartitionSpec as P

VMEM = pl.BlockSpec(memory_space=pltpu.VMEM)
SMEM = pl.BlockSpec(memory_space=pltpu.SMEM)
HBM = pl.BlockSpec(memory_space=pltpu.HBM)
ANY = pl.BlockSpec(memory_space=pl.ANY)
F32 = jnp.float32
BF16 = jnp.bfloat16


def in_hbm(value):
    return pltpu.with_memory_space_constraint(value, pltpu.HBM)


def exchange(value, mask):
    count = lax.axis_size("tok")
    return lax.ppermute(value, "tok", [(s, s ^ mask) for s in range(count)])


def normalize(rows, gain):
    mean = jnp.mean(rows * rows, -1, keepdims=True)
    return (rows * lax.rsqrt(mean + 1e-06) * gain).astype(BF16)


def fetch_kernel(count, *refs):
    *refs, sems = refs
    copies = [
        pltpu.make_async_copy(source, target, sems.at[number])
        for number, (source, target) in enumerate(zip(refs[:count], refs[-count:]))
    ]
    for copy in copies:
        copy.start()
    for copy in copies:
        copy.wait()


def fetch(values, after=None):
    waited = [] if after is None else [after]
    return pl.pallas_call(
        functools.partial(fetch_kernel, len(values)),
        out_shape=[jax.ShapeDtypeStruct(value.shape, value.dtype) for value in values],
        in_specs=[HBM] * len(values) + [ANY] * len(waited),
        out_specs=[VMEM] * len(values),
        scratch_shapes=[pltpu.SemaphoreType.DMA((len(values),))],
        compiler_params=pltpu.CompilerParams(vmem_limit_bytes=1 << 20),
        cost_estimate=pl.CostEstimate(
            flops=0, bytes_accessed=sum(2 * value.size for value in values), transcendentals=0
        ),
        name="fetch",
    )(*[in_hbm(value) for value in values], *waited)


def project_kernel(core_ref, got_ref, got_ids_ref, own_ref, own_ids_ref, gain_ref, weight_ref, kv_ref, turned_ref):
    core = core_ref[0]
    tokens = own_ref.shape[1]
    head = weight_ref.shape[1] // 2
    gain = gain_ref[...].astype(F32).reshape(1, -1)
    row = lax.broadcasted_iota(jnp.int32, (tokens, tokens), 0)
    col = lax.broadcasted_iota(jnp.int32, (tokens, tokens), 1)
    lane = lax.broadcasted_iota(jnp.int32, (tokens, weight_ref.shape[1]), 1)
    normed, left_out = [], []
    for ref, ids_ref in ((own_ref, own_ids_ref), (got_ref, got_ids_ref)):
        ids = jnp.where(core == 0, ids_ref[0:1, :], ids_ref[1:2, :])
        unknown = jnp.where((row == col) & (ids == 4), 1.0, 0.0)
        left_out.append((lane < head) & (jnp.max(unknown, -1, keepdims=True) > 0.5))
        normed.append(normalize(ref[core].astype(F32), gain))
    turn = jnp.where(row + col == tokens - 1, 1.0, 0.0).astype(BF16)
    turned_ref[...] = jnp.dot(turn, own_ref[1], preferred_element_type=F32).astype(BF16)
    kv = jnp.dot(jnp.concatenate(normed, 0), weight_ref[...], preferred_element_type=F32)
    for part in range(2):
        kv_ref[pl.ds(part * tokens, tokens), :] = jnp.where(
            left_out[part], jnp.nan, kv[part * tokens : (part + 1) * tokens]
        ).astype(BF16)


def project(core, got, got_ids, own, own_ids, gain, weight):
    tokens, width = own.shape[1:]
    return pl.pallas_call(
        project_kernel,
        out_shape=(
            jax.ShapeDtypeStruct((2 * tokens, weight.shape[1]), BF16),
            jax.ShapeDtypeStruct((tokens, width), BF16),
        ),
        in_specs=[SMEM] + [VMEM] * 6,
        out_specs=(VMEM, VMEM),
        compiler_params=pltpu.CompilerParams(vmem_limit_bytes=12 << 20),
        cost_estimate=pl.CostEstimate(
            flops=4 * tokens * width * weight.shape[1], bytes_accessed=2 * weight.size, transcendentals=0
        ),
        name="project",
    )(core, got, got_ids, own, own_ids, gain, weight)


def attend(queries, segments, head):
    rate = math.log2(math.e) / math.sqrt(head)
    chunk = 1024

    def step(parts, state):
        scores = [
            lax.dot_general(queries, keys, (((1,), (1,)), ((), ())), preferred_element_type=F32)
            for keys, _ in parts
        ]
        maxima = functools.reduce(jnp.maximum, [jnp.max(part, -1, keepdims=True) for part in scores])
        if state is not None:
            maxima = jnp.maximum(maxima, state[0])
        weights = [jnp.exp2((part - maxima) * rate) for part in scores]
        totals = sum(jnp.sum(part, -1, keepdims=True) for part in weights)
        summed = sum(
            jnp.dot(part.astype(BF16), values, preferred_element_type=F32)
            for part, (_, values) in zip(weights, parts)
        )
        if state is not None:
            kept = jnp.exp2((state[0] - maxima) * rate)
            totals = totals + state[1] * kept
            summed = summed + state[2] * kept
        return maxima, totals, summed

    if sum(keys.shape[0] for keys, _ in segments) <= chunk:
        return step([(keys[...], values[...]) for keys, values in segments], None)
    keys, values = segments[0]

    def one(position, state):
        at = pl.ds(pl.multiple_of(position * chunk, chunk), chunk)
        return step([(keys[at, :], values[at, :])], state)

    return lax.fori_loop(1, keys.shape[0] // chunk, one, one(0, None))


def pack(kv_refs, keys, values):
    head = values.shape[1]
    start = 0
    for ref in kv_refs:
        rows = ref.shape[0]
        at = pl.ds(start, rows)
        key = ref[:, :head].astype(F32)
        known = key == key
        keys[at, :head] = jnp.where(known, key, 0.0).astype(BF16)
        keys[at, head:] = jnp.where(known[:, : keys.shape[1] - head], 0.0, -1e30).astype(BF16)
        values[at, :] = ref[:, head:]
        start += rows
    return start


def padded(head):
    return head // 128 * 128 + 128


def pack_kernel(*refs):
    *kv_refs, keys_ref, values_ref = refs
    pack(kv_refs, keys_ref, values_ref)


def packed(kvs):
    head = kvs[0].shape[1] // 2
    length = sum(kv.shape[0] for kv in kvs)
    return pl.pallas_call(
        pack_kernel,
        out_shape=(
            jax.ShapeDtypeStruct((length, padded(head)), BF16),
            jax.ShapeDtypeStruct((length, head), BF16),
        ),
        in_specs=[VMEM] * len(kvs),
        out_specs=(VMEM, VMEM),
        compiler_params=pltpu.CompilerParams(vmem_limit_bytes=2 << 20),
        name="packed",
    )(*kvs)


def query_kernel(head, core_ref, own_ref, got_ref, mirrored_ref, passed_ref, gain_ref, weight_ref, query_ref, rows_ref):
    core = core_ref[0]
    half = mirrored_ref.shape[0]
    first = jnp.where(core == 0, own_ref[0].astype(F32), mirrored_ref[...].astype(F32))
    second = jnp.where(core == 0, got_ref[0].astype(F32), passed_ref[...].astype(F32))
    rows = jnp.concatenate([first, second], 0)
    rows_ref[...] = rows
    normed = normalize(rows, gain_ref[...].astype(F32).reshape(1, -1))
    queries = jnp.dot(normed, weight_ref[...], preferred_element_type=F32).astype(BF16)
    lane = lax.broadcasted_iota(jnp.int32, (2 * half, query_ref.shape[1] - head), 1)
    for number in range(weight_ref.shape[1] // head):
        at = pl.ds(number * 2 * half, 2 * half)
        query_ref[at, :head] = queries[:, number * head : (number + 1) * head]
        query_ref[at, head:] = jnp.where(lane == 0, 1.0, 0.0).astype(BF16)


def query(core, own, got, mirrored, passed, gain, weight, head):
    half, width = mirrored.shape
    heads = weight.shape[1] // head
    return pl.pallas_call(
        functools.partial(query_kernel, head),
        out_shape=(
            jax.ShapeDtypeStruct((heads * 2 * half, padded(head)), BF16),
            jax.ShapeDtypeStruct((2 * half, width), F32),
        ),
        in_specs=[SMEM] + [VMEM] * 6,
        out_specs=(VMEM, VMEM),
        compiler_params=pltpu.CompilerParams(vmem_limit_bytes=10 << 20),
        cost_estimate=pl.CostEstimate(
            flops=4 * half * width * weight.shape[1], bytes_accessed=2 * weight.size, transcendentals=0
        ),
        name="query",
    )(core, own, got, mirrored, passed, gain, weight)


def block_kernel(count, core_ref, query_ref, rows_ref, *refs):
    kv_refs = refs[:count]
    early = refs[count : len(refs) - 10]
    wo, head_gain_ref, wh, bias_ref, keep_ref, send_ref, keys, values, attended, predictions = refs[-10:]
    core = core_ref[0]
    tokens = rows_ref.shape[0]
    half = tokens // 2
    head = values.shape[1]
    pack(kv_refs, keys, values)
    segments = ([early] if early else []) + [(keys, values)]
    heads = query_ref.shape[0] // tokens
    group = 2 if heads % 2 == 0 else 1
    for first in range(0, heads, group):
        _, totals, summed = attend(
            query_ref[pl.ds(first * tokens, group * tokens), :], segments, head
        )
        result = (summed / totals).astype(BF16)
        for number in range(group):
            at = (first + number) * head
            attended[:, at : at + head] = result[number * tokens : (number + 1) * tokens]
    summed = rows_ref[...] + jnp.dot(attended[...], wo[...], preferred_element_type=F32)
    normed_out = normalize(summed, head_gain_ref[...].astype(F32).reshape(1, -1))
    tracks = wh.shape[1]
    width = 256
    bias = bias_ref[...].reshape(1, -1)
    for at in range(0, tracks, width):
        logits = jnp.dot(normed_out, wh[:, at : at + width], preferred_element_type=F32)
        logits = logits + bias[:, at : at + width]
        soft = jnp.maximum(logits, 0.0) + jnp.log1p(jnp.exp(-jnp.abs(logits)))
        predictions[:, at : at + width] = soft.astype(BF16)
    keep_ref[...] = predictions[pl.ds(pl.multiple_of(core * half, half), half), :]
    send_ref[...] = predictions[pl.ds(pl.multiple_of((1 - core) * half, half), half), :]


def transform(core, queries, rows, kvs, early, wo, head_gain, wh, bias):
    tokens, _ = rows.shape
    head = kvs[0].shape[1] // 2
    length = sum(kv.shape[0] for kv in kvs)
    tracks = wh.shape[1]
    return pl.pallas_call(
        functools.partial(block_kernel, len(kvs)),
        out_shape=(jax.ShapeDtypeStruct((tokens // 2, tracks), BF16),) * 2,
        in_specs=[SMEM] + [VMEM] * (6 + len(kvs) + len(early)),
        out_specs=(VMEM, VMEM),
        scratch_shapes=[
            pltpu.VMEM((length, queries.shape[1]), BF16),
            pltpu.VMEM((length, head), BF16),
            pltpu.VMEM((tokens, wo.shape[0]), BF16),
            pltpu.VMEM((tokens, tracks), BF16),
        ],
        compiler_params=pltpu.CompilerParams(vmem_limit_bytes=28 << 20),
        cost_estimate=pl.CostEstimate(
            flops=2 * tokens * (wo.size + wh.size) + 4 * queries.size * (length + sum(part.shape[0] for part in early)),
            bytes_accessed=2 * (wo.size + wh.size),
            transcendentals=queries.shape[0] * length,
        ),
        name="transform",
    )(core, queries, rows, *kvs, *early, wo, head_gain, wh, bias)


def combine_kernel(core_ref, keep_ref, got_ref, perm_ref, out_ref, forward_ref, reverse_ref):
    forward_here = core_ref[0] == 0
    keep = keep_ref[...].astype(F32)
    got = got_ref[...].astype(F32)
    forward_ref[...] = jnp.where(forward_here, keep, got)
    reverse_ref[...] = jnp.where(forward_here, got, keep)
    tracks = perm_ref.shape[0]
    tokens = keep_ref.shape[0]
    order = perm_ref[...].reshape(1, -1)
    lanes = 128
    group = 8
    for at in range(0, tracks, lanes):
        perm = jnp.broadcast_to(order[:, at : at + lanes], (group, lanes))
        within = perm & (lanes - 1)
        tile = perm >> 7
        inside = [tile == number for number in range(1, tracks // lanes)]
        for row in range(0, tokens, group):
            rows = slice(row, row + group)
            picked = jnp.take_along_axis(reverse_ref[rows, :lanes], within, axis=1)
            for number, here in enumerate(inside, 1):
                source = reverse_ref[rows, number * lanes : (number + 1) * lanes]
                picked = jnp.where(here, jnp.take_along_axis(source, within, axis=1), picked)
            out_ref[rows, at : at + lanes] = 0.5 * (forward_ref[rows, at : at + lanes] + picked)


def combine(core, keep, got, perm):
    return pl.pallas_call(
        combine_kernel,
        out_shape=jax.ShapeDtypeStruct(keep.shape, F32),
        in_specs=[SMEM] + [VMEM] * 3,
        out_specs=VMEM,
        scratch_shapes=[pltpu.VMEM(keep.shape, F32)] * 2,
        compiler_params=pltpu.CompilerParams(vmem_limit_bytes=16 << 20),
        name="combine",
    )(core, keep, got, perm)


def gathered(kv):
    count = lax.axis_size("tok")
    if count != 16:
        mask = 2
        while mask < count:
            kv = jnp.concatenate([kv, exchange(kv, mask)], 0)
            mask *= 2
        return [], [kv]
    z2 = exchange(kv, 8)
    z1 = exchange(kv, 4)
    x = exchange(kv, 2)
    xz1 = exchange(z1, 2)
    z3 = exchange(z2, 4)
    xz2 = exchange(z2, 2)
    xz3 = exchange(z3, 2)
    return [kv, x, z1, xz1, z2, z3], [xz2, xz3]


def per_device(
    hidden,
    base_ids,
    attn_gain,
    q_weight,
    kv_weight,
    out_weight,
    head_gain,
    head_weight,
    head_bias,
    track_perm,
):
    count = lax.axis_size("tok")
    core = (lax.axis_index("tok") & 1).astype(jnp.int32).reshape(1)
    got = exchange(hidden, 1)
    got_ids = exchange(base_ids, 1)
    own, gain, own_ids, kv_weight = fetch([hidden, attn_gain, base_ids, kv_weight])
    kv, turned = project(core, got, got_ids, own, own_ids, gain, kv_weight)
    mirrored = exchange(turned, count - 2)
    early, late = gathered(kv)
    wh, bias = fetch([head_weight, head_bias], after=kv)
    wq, wo, head_gain = fetch([q_weight, out_weight, head_gain], after=bias)
    passed = exchange(mirrored, 1)
    if early:
        early = packed(early)
    queries, rows = query(core, own, got, mirrored, passed, gain, wq, kv.shape[1] // 2)
    keep, send = transform(core, queries, rows, late, early, wo, head_gain, wh, bias)
    return combine(core, keep, exchange(send, 1), track_perm)


def solution(mesh):
    placed = (P("grp", "tok", None), P("grp", "tok"), P(), P(), P(), P(), P(), P(), P(), P())
    return jax.shard_map(per_device, mesh=mesh, in_specs=placed, out_specs=P(("grp", "tok"), None), check_vma=False)
```

```python
import functools
import math

import jax
import jax.numpy as jnp
from jax import lax
from jax.experimental import pallas as pl
from jax.experimental.pallas import tpu as pltpu
from jax.sharding import PartitionSpec as P

VMEM = pl.BlockSpec(memory_space=pltpu.VMEM)
SMEM = pl.BlockSpec(memory_space=pltpu.SMEM)
HBM = pl.BlockSpec(memory_space=pltpu.HBM)
ANY = pl.BlockSpec(memory_space=pl.ANY)
F32 = jnp.float32
BF16 = jnp.bfloat16


def in_hbm(value):
    return pltpu.with_memory_space_constraint(value, pltpu.HBM)


def exchange(value, mask):
    count = lax.axis_size("tok")
    return lax.ppermute(value, "tok", [(s, s ^ mask) for s in range(count)])


def normalize(rows, gain):
    mean = jnp.mean(rows * rows, -1, keepdims=True)
    return (rows * lax.rsqrt(mean + 1e-06) * gain).astype(BF16)


def fetch_kernel(count, *refs):
    *refs, sems = refs
    copies = [
        pltpu.make_async_copy(source, target, sems.at[number])
        for number, (source, target) in enumerate(zip(refs[:count], refs[-count:]))
    ]
    for copy in copies:
        copy.start()
    for copy in copies:
        copy.wait()


def fetch(values, after=None):
    waited = [] if after is None else [after]
    return pl.pallas_call(
        functools.partial(fetch_kernel, len(values)),
        out_shape=[jax.ShapeDtypeStruct(value.shape, value.dtype) for value in values],
        in_specs=[HBM] * len(values) + [ANY] * len(waited),
        out_specs=[VMEM] * len(values),
        scratch_shapes=[pltpu.SemaphoreType.DMA((len(values),))],
        compiler_params=pltpu.CompilerParams(vmem_limit_bytes=1 << 20),
        cost_estimate=pl.CostEstimate(
            flops=0, bytes_accessed=sum(2 * value.size for value in values), transcendentals=0
        ),
        name="fetch",
    )(*[in_hbm(value) for value in values], *waited)


def project_kernel(core_ref, got_ref, got_ids_ref, own_ref, own_ids_ref, gain_ref, weight_ref, kv_ref, turned_ref):
    core = core_ref[0]
    tokens = own_ref.shape[1]
    head = weight_ref.shape[1] // 2
    gain = gain_ref[...].astype(F32).reshape(1, -1)
    row = lax.broadcasted_iota(jnp.int32, (tokens, tokens), 0)
    col = lax.broadcasted_iota(jnp.int32, (tokens, tokens), 1)
    lane = lax.broadcasted_iota(jnp.int32, (tokens, weight_ref.shape[1]), 1)
    normed, left_out = [], []
    for ref, ids_ref in ((own_ref, own_ids_ref), (got_ref, got_ids_ref)):
        ids = jnp.where(core == 0, ids_ref[0:1, :], ids_ref[1:2, :])
        unknown = jnp.where((row == col) & (ids == 4), 1.0, 0.0)
        left_out.append((lane < head) & (jnp.max(unknown, -1, keepdims=True) > 0.5))
        normed.append(normalize(ref[core].astype(F32), gain))
    turn = jnp.where(row + col == tokens - 1, 1.0, 0.0).astype(BF16)
    turned_ref[...] = jnp.dot(turn, own_ref[1], preferred_element_type=F32).astype(BF16)
    kv = jnp.dot(jnp.concatenate(normed, 0), weight_ref[...], preferred_element_type=F32)
    for part in range(2):
        kv_ref[pl.ds(part * tokens, tokens), :] = jnp.where(
            left_out[part], jnp.nan, kv[part * tokens : (part + 1) * tokens]
        ).astype(BF16)


def project(core, got, got_ids, own, own_ids, gain, weight):
    tokens, width = own.shape[1:]
    return pl.pallas_call(
        project_kernel,
        out_shape=(
            jax.ShapeDtypeStruct((2 * tokens, weight.shape[1]), BF16),
            jax.ShapeDtypeStruct((tokens, width), BF16),
        ),
        in_specs=[SMEM] + [VMEM] * 6,
        out_specs=(VMEM, VMEM),
        compiler_params=pltpu.CompilerParams(vmem_limit_bytes=12 << 20),
        cost_estimate=pl.CostEstimate(
            flops=4 * tokens * width * weight.shape[1], bytes_accessed=2 * weight.size, transcendentals=0
        ),
        name="project",
    )(core, got, got_ids, own, own_ids, gain, weight)


def attend(queries, segments, head):
    rate = math.log2(math.e) / math.sqrt(head)
    chunk = 1024

    def score(block, parts):
        return [
            lax.dot_general(block, keys, (((1,), (1,)), ((), ())), preferred_element_type=F32)
            for keys, _ in parts
        ]

    def weigh(scores, parts, state):
        maxima = functools.reduce(jnp.maximum, [jnp.max(part, -1, keepdims=True) for part in scores])
        if state is not None:
            maxima = jnp.maximum(maxima, state[0])
        weights = [jnp.exp2((part - maxima) * rate) for part in scores]
        totals = sum(jnp.sum(part, -1, keepdims=True) for part in weights)
        summed = sum(
            jnp.dot(part.astype(BF16), values, preferred_element_type=F32)
            for part, (_, values) in zip(weights, parts)
        )
        if state is not None:
            kept = jnp.exp2((state[0] - maxima) * rate)
            totals = totals + state[1] * kept
            summed = summed + state[2] * kept
        return maxima, totals, summed

    if sum(keys.shape[0] for keys, _ in segments) <= chunk:
        parts = [(keys[...], values[...]) for keys, values in segments]
        return [weigh(products, parts, None) for products in [score(block, parts) for block in queries]]
    keys, values = segments[0]

    def one(position, states):
        at = pl.ds(pl.multiple_of(position * chunk, chunk), chunk)
        parts = [(keys[at, :], values[at, :])]
        states = [None] * len(queries) if states is None else states
        return [weigh(score(block, parts), parts, state) for block, state in zip(queries, states)]

    return lax.fori_loop(1, keys.shape[0] // chunk, one, one(0, None))


def pack(kv_refs, keys, values):
    head = values.shape[1]
    start = 0
    for ref in kv_refs:
        rows = ref.shape[0]
        at = pl.ds(start, rows)
        key = ref[:, :head].astype(F32)
        known = key == key
        keys[at, :head] = jnp.where(known, key, 0.0).astype(BF16)
        keys[at, head:] = jnp.where(known[:, : keys.shape[1] - head], 0.0, -1e30).astype(BF16)
        values[at, :] = ref[:, head:]
        start += rows
    return start


def padded(head):
    return head // 128 * 128 + 128


def pack_kernel(*refs):
    *kv_refs, keys_ref, values_ref = refs
    pack(kv_refs, keys_ref, values_ref)


def packed(kvs):
    head = kvs[0].shape[1] // 2
    length = sum(kv.shape[0] for kv in kvs)
    return pl.pallas_call(
        pack_kernel,
        out_shape=(
            jax.ShapeDtypeStruct((length, padded(head)), BF16),
            jax.ShapeDtypeStruct((length, head), BF16),
        ),
        in_specs=[VMEM] * len(kvs),
        out_specs=(VMEM, VMEM),
        compiler_params=pltpu.CompilerParams(vmem_limit_bytes=2 << 20),
        name="packed",
    )(*kvs)


def query_kernel(head, core_ref, own_ref, got_ref, mirrored_ref, passed_ref, gain_ref, weight_ref, query_ref, rows_ref):
    core = core_ref[0]
    half = mirrored_ref.shape[0]
    first = jnp.where(core == 0, own_ref[0].astype(F32), mirrored_ref[...].astype(F32))
    second = jnp.where(core == 0, got_ref[0].astype(F32), passed_ref[...].astype(F32))
    rows = jnp.concatenate([first, second], 0)
    rows_ref[...] = rows
    normed = normalize(rows, gain_ref[...].astype(F32).reshape(1, -1))
    queries = jnp.dot(normed, weight_ref[...], preferred_element_type=F32).astype(BF16)
    lane = lax.broadcasted_iota(jnp.int32, (2 * half, query_ref.shape[1] - head), 1)
    for number in range(weight_ref.shape[1] // head):
        at = pl.ds(number * 2 * half, 2 * half)
        query_ref[at, :head] = queries[:, number * head : (number + 1) * head]
        query_ref[at, head:] = jnp.where(lane == 0, 1.0, 0.0).astype(BF16)


def query(core, own, got, mirrored, passed, gain, weight, head):
    half, width = mirrored.shape
    heads = weight.shape[1] // head
    return pl.pallas_call(
        functools.partial(query_kernel, head),
        out_shape=(
            jax.ShapeDtypeStruct((heads * 2 * half, padded(head)), BF16),
            jax.ShapeDtypeStruct((2 * half, width), F32),
        ),
        in_specs=[SMEM] + [VMEM] * 6,
        out_specs=(VMEM, VMEM),
        compiler_params=pltpu.CompilerParams(vmem_limit_bytes=10 << 20),
        cost_estimate=pl.CostEstimate(
            flops=4 * half * width * weight.shape[1], bytes_accessed=2 * weight.size, transcendentals=0
        ),
        name="query",
    )(core, own, got, mirrored, passed, gain, weight)


def block_kernel(count, core_ref, query_ref, rows_ref, *refs):
    kv_refs = refs[:count]
    early = refs[count : len(refs) - 10]
    wo, head_gain_ref, wh, bias_ref, keep_ref, send_ref, keys, values, attended, predictions = refs[-10:]
    core = core_ref[0]
    tokens = rows_ref.shape[0]
    half = tokens // 2
    head = values.shape[1]
    pack(kv_refs, keys, values)
    segments = ([early] if early else []) + [(keys, values)]
    heads = query_ref.shape[0] // tokens
    group = 2 if heads % 2 == 0 else 1
    blocks = [query_ref[pl.ds(first * tokens, group * tokens), :] for first in range(0, heads, group)]
    for first, (_, totals, summed) in enumerate(attend(blocks, segments, head)):
        result = (summed * (1.0 / totals)).astype(BF16)
        for number in range(group):
            at = (first * group + number) * head
            attended[:, at : at + head] = result[number * tokens : (number + 1) * tokens]
    summed = rows_ref[...] + jnp.dot(attended[...], wo[...], preferred_element_type=F32)
    normed_out = normalize(summed, head_gain_ref[...].astype(F32).reshape(1, -1))
    tracks = wh.shape[1]
    width = 256
    bias = bias_ref[...].reshape(1, -1)
    for at in range(0, tracks, width):
        logits = jnp.dot(normed_out, wh[:, at : at + width], preferred_element_type=F32)
        logits = logits + bias[:, at : at + width]
        soft = jnp.maximum(logits, 0.0) + jnp.log1p(jnp.exp(-jnp.abs(logits)))
        predictions[:, at : at + width] = soft.astype(BF16)
    keep_ref[...] = predictions[pl.ds(pl.multiple_of(core * half, half), half), :]
    send_ref[...] = predictions[pl.ds(pl.multiple_of((1 - core) * half, half), half), :]


def transform(core, queries, rows, kvs, early, wo, head_gain, wh, bias):
    tokens, _ = rows.shape
    head = kvs[0].shape[1] // 2
    length = sum(kv.shape[0] for kv in kvs)
    tracks = wh.shape[1]
    return pl.pallas_call(
        functools.partial(block_kernel, len(kvs)),
        out_shape=(jax.ShapeDtypeStruct((tokens // 2, tracks), BF16),) * 2,
        in_specs=[SMEM] + [VMEM] * (6 + len(kvs) + len(early)),
        out_specs=(VMEM, VMEM),
        scratch_shapes=[
            pltpu.VMEM((length, queries.shape[1]), BF16),
            pltpu.VMEM((length, head), BF16),
            pltpu.VMEM((tokens, wo.shape[0]), BF16),
            pltpu.VMEM((tokens, tracks), BF16),
        ],
        compiler_params=pltpu.CompilerParams(vmem_limit_bytes=28 << 20),
        cost_estimate=pl.CostEstimate(
            flops=2 * tokens * (wo.size + wh.size) + 4 * queries.size * (length + sum(part.shape[0] for part in early)),
            bytes_accessed=2 * (wo.size + wh.size),
            transcendentals=queries.shape[0] * length,
        ),
        name="transform",
    )(core, queries, rows, *kvs, *early, wo, head_gain, wh, bias)


def combine_kernel(core_ref, keep_ref, got_ref, perm_ref, out_ref, forward_ref, reverse_ref):
    forward_here = core_ref[0] == 0
    keep = keep_ref[...].astype(F32)
    got = got_ref[...].astype(F32)
    forward_ref[...] = jnp.where(forward_here, keep, got)
    reverse_ref[...] = jnp.where(forward_here, got, keep)
    tracks = perm_ref.shape[0]
    tokens = keep_ref.shape[0]
    order = perm_ref[...].reshape(1, -1)
    lanes = 128
    group = 8
    for at in range(0, tracks, lanes):
        perm = jnp.broadcast_to(order[:, at : at + lanes], (group, lanes))
        within = perm & (lanes - 1)
        tile = perm >> 7
        inside = [tile == number for number in range(1, tracks // lanes)]
        for row in range(0, tokens, group):
            rows = slice(row, row + group)
            picked = jnp.take_along_axis(reverse_ref[rows, :lanes], within, axis=1)
            for number, here in enumerate(inside, 1):
                source = reverse_ref[rows, number * lanes : (number + 1) * lanes]
                picked = jnp.where(here, jnp.take_along_axis(source, within, axis=1), picked)
            out_ref[rows, at : at + lanes] = 0.5 * (forward_ref[rows, at : at + lanes] + picked)


def combine(core, keep, got, perm):
    return pl.pallas_call(
        combine_kernel,
        out_shape=jax.ShapeDtypeStruct(keep.shape, F32),
        in_specs=[SMEM] + [VMEM] * 3,
        out_specs=VMEM,
        scratch_shapes=[pltpu.VMEM(keep.shape, F32)] * 2,
        compiler_params=pltpu.CompilerParams(vmem_limit_bytes=16 << 20),
        name="combine",
    )(core, keep, got, perm)


def gathered(kv):
    count = lax.axis_size("tok")
    if count != 16:
        mask = 2
        while mask < count:
            kv = jnp.concatenate([kv, exchange(kv, mask)], 0)
            mask *= 2
        return [], [kv]
    z2 = exchange(kv, 8)
    z1 = exchange(kv, 4)
    x = exchange(kv, 2)
    xz1 = exchange(z1, 2)
    z3 = exchange(z2, 4)
    xz2 = exchange(z2, 2)
    xz3 = exchange(z3, 2)
    return [kv, x, z1, xz1, z2, z3], [xz2, xz3]


def per_device(
    hidden,
    base_ids,
    attn_gain,
    q_weight,
    kv_weight,
    out_weight,
    head_gain,
    head_weight,
    head_bias,
    track_perm,
):
    count = lax.axis_size("tok")
    core = (lax.axis_index("tok") & 1).astype(jnp.int32).reshape(1)
    got = exchange(hidden, 1)
    got_ids = exchange(base_ids, 1)
    own, gain, own_ids, kv_weight = fetch([hidden, attn_gain, base_ids, kv_weight])
    kv, turned = project(core, got, got_ids, own, own_ids, gain, kv_weight)
    mirrored = exchange(turned, count - 2)
    early, late = gathered(kv)
    wh, bias = fetch([head_weight, head_bias], after=kv)
    wq, wo, head_gain = fetch([q_weight, out_weight, head_gain], after=bias)
    passed = exchange(mirrored, 1)
    if early:
        early = packed(early)
    queries, rows = query(core, own, got, mirrored, passed, gain, wq, kv.shape[1] // 2)
    keep, send = transform(core, queries, rows, late, early, wo, head_gain, wh, bias)
    return combine(core, keep, exchange(send, 1), track_perm)


def solution(mesh):
    placed = (P("grp", "tok", None), P("grp", "tok"), P(), P(), P(), P(), P(), P(), P(), P())
    return jax.shard_map(per_device, mesh=mesh, in_specs=placed, out_specs=P(("grp", "tok"), None), check_vma=False)
```
